128 devices in a mesh: ty: 8 (over x, core), tx: 16 (over z, y).
Axes of the slice: x: 4, y: 4, z: 4, core: 2. Of those that a mesh axis runs over, the one named last changes fastest.
Arguments:
- spectrum: float32 [2, 4096, 8192], P(None, 'ty', 'tx')
- measured: float32 [128, 256, 256], P(('ty', 'tx')), may hold values from 0.5 to 6
- pupil_mask: int32 [256, 256], replicated, may hold values 0 or 1
- led_count: int32 [128], replicated, may hold values from 4 to 8, as said below
- led_owner: int32 [128, 8], replicated, may hold values from 0 to 15, as said below
- led_offset: int32 [128, 8, 2], replicated, may hold values from 0 to 256
Outputs:
- spectrum_step: float32 [2, 4096, 8192], P(None, 'ty', 'tx')
- cg_residual: float32 [2, 4096, 8192], P(None, 'ty', 'tx')
The draws below stay inside these ranges and needn't reach their ends.
Inputs may be any that keep to these rules, and one draw needn't show every extreme that they name: Capture c lights the LEDs of slots 0 to led_count[c] - 1; some capture lights 8 in every draw. `led_owner`: for capture c, taken on device (c // 16, c % 16) of the mesh (ty, tx), slot t names the column of the tile in tile row c // 16 that holds the slot's block. The live slots of one capture name distinct tiles. No tile holds the blocks of more than 8 live slots over the captures of its tile row, and in every tile row some tile holds exactly 8. `led_offset`: every block lies inside the tile named by led_owner.
All inputs are finite; a program needn't handle non-finite values.
Results may differ from the reference program's by a relative error of at most 0.0003.
Values sent between devices are 32-bit elements; how exact they have to be, the bound alone decides.
A program may use at most 128 MiB of HBM per device.

```python
import jax
import jax.numpy as jnp
from jax import lax

B = 256
TILE_R = 512
TILE_C = 512
LED_MOST = 8
ITERS = 2
CAPTURES = 128
ROWS_ALL = 4096
COLS_ALL = 8192
N_TY = 8
N_TX = 16


def draw_spectrum(key, part):
    keys = jax.random.split(key, 3)
    base = jax.random.normal(keys[0], (2, ROWS_ALL, COLS_ALL), jnp.float32)
    row_ramp = jnp.exp(jnp.arange(ROWS_ALL, dtype=jnp.float32) * (0.55 / ROWS_ALL))
    col_ramp = jnp.exp(jnp.arange(COLS_ALL, dtype=jnp.float32) * (0.55 / COLS_ALL))
    row_jitter = jnp.exp(jax.random.uniform(keys[1], (ROWS_ALL,), jnp.float32, 0.0, 0.5))
    col_jitter = jnp.exp(jax.random.uniform(keys[2], (COLS_ALL,), jnp.float32, 0.0, 0.5))
    rows_scale = row_ramp * row_jitter
    cols_scale = col_ramp * col_jitter
    return 0.25 * base * rows_scale[None, :, None] * cols_scale[None, None, :]


def led_layout(key):
    count_key = jax.random.fold_in(key, 101)
    place_key = jax.random.fold_in(key, 202)
    tile_key = jax.random.fold_in(key, 303)
    start_key = jax.random.fold_in(key, 404)
    counts = jax.random.randint(count_key, (N_TY, N_TX), 4, LED_MOST + 1)
    columns = jnp.arange(N_TX, dtype=jnp.int32)[None, :]
    place_scores = jax.random.randint(place_key, (N_TY, N_TX), 0, 1 << 20) * N_TX + columns
    tile_scores = jax.random.randint(tile_key, (N_TY, N_TX), 0, 1 << 20) * N_TX + columns
    position = jnp.argsort(jnp.argsort(place_scores, axis=1, stable=True), axis=1, stable=True).astype(jnp.int32)
    tile_order = jnp.argsort(tile_scores, axis=1, stable=True).astype(jnp.int32)
    run_start = jax.random.randint(start_key, (N_TY, 1), 0, N_TX)
    distance = (position - run_start) % N_TX
    counts = jnp.where(distance < LED_MOST, jnp.maximum(counts, LED_MOST - distance), counts)
    slot_ids = jnp.arange(LED_MOST, dtype=jnp.int32)
    lookup = ((position[:, :, None] + slot_ids[None, None, :]) % N_TX).reshape(N_TY, N_TX * LED_MOST)
    owners = jnp.take_along_axis(tile_order, lookup, axis=1)
    return (counts.reshape(CAPTURES).astype(jnp.int32), owners.reshape(CAPTURES, LED_MOST).astype(jnp.int32))


def draw_led_count(key, part):
    return led_layout(key)[0]


def draw_led_owner(key, part):
    return led_layout(key)[1]


def set_ends(values, key, least, top_value):
    extent = values.shape
    index_at = [jax.random.randint(jax.random.fold_in(key, axis), (), 0, extent[axis]) for axis in range(len(extent))]
    values = values.at[tuple(index_at)].set(least)
    longest = extent.index(max(extent))
    index_at[longest] = (index_at[longest] + 1) % extent[longest]
    return values.at[tuple(index_at)].set(top_value)


def block_scale(key, dims, pieces, low, largest):
    def one(axis_at, shards_of):
        heights = jax.random.uniform(jax.random.fold_in(jax.random.fold_in(key, 6), axis_at), (shards_of,), jnp.float32, low / len(pieces), largest / len(pieces))
        return jnp.repeat(jnp.exp(heights), dims[axis_at] // shards_of).reshape((-1,) + (1,) * (len(dims) - axis_at - 1))

    loudness = one(*pieces[0])
    for cut in pieces[1:]:
        loudness = loudness * one(*cut)
    return loudness


def setup_inputs(seed: int = 0) -> dict:
    key_list = jax.random.split(jax.random.key(seed), 7)
    spectrum = draw_spectrum(jax.random.fold_in(key_list[6], 71), 0)
    measured = jnp.clip(0.5 + 5.5 * jax.random.uniform(key_list[1], (CAPTURES, B, B), jnp.float32) ** block_scale(key_list[1], (CAPTURES, B, B), ((0, 128),), -0.2, 0.2), 0.5, 6.0)
    pupil_mask = set_ends((jax.random.randint(key_list[2], (B, B), 0, 4) < 3).astype(jnp.int32), jax.random.fold_in(key_list[2], 1), 0, 1)
    led_count = draw_led_count(jax.random.fold_in(key_list[6], 71), 0)
    led_owner = draw_led_owner(jax.random.fold_in(key_list[6], 71), 0)
    led_offset = set_ends(jax.random.randint(key_list[5], (CAPTURES, LED_MOST, 2), 0, min(TILE_R, TILE_C) - B + 1), jax.random.fold_in(key_list[5], 1), 0, min(TILE_R, TILE_C) - B).astype(jnp.int32)
    return {"spectrum": spectrum, "measured": measured, "pupil_mask": pupil_mask, "led_count": led_count, "led_owner": led_owner, "led_offset": led_offset}


REG = 0.5

def dft_tables(side_len):
    indices = jnp.arange(side_len, dtype=jnp.int32)
    product = indices[:, None] * indices[None, :] % side_len
    angles = product.astype(jnp.float32) * (2.0 * jnp.pi / side_len)
    scale_one = 1.0 / jnp.sqrt(jnp.asarray(side_len, jnp.float32))
    return (jnp.cos(angles) * scale_one, jnp.sin(angles) * scale_one)

def transform(real_part, imag_part, cosine_table, sine_table, orient):
    highest = lax.Precision.HIGHEST
    left_real = jnp.einsum('jk,skl->sjl', cosine_table, real_part, precision=highest) - orient * jnp.einsum('jk,skl->sjl', sine_table, imag_part, precision=highest)
    left_imag = jnp.einsum('jk,skl->sjl', cosine_table, imag_part, precision=highest) + orient * jnp.einsum('jk,skl->sjl', sine_table, real_part, precision=highest)
    out_real = jnp.einsum('sjk,kl->sjl', left_real, cosine_table, precision=highest) - orient * jnp.einsum('sjk,kl->sjl', left_imag, sine_table, precision=highest)
    out_imag = jnp.einsum('sjk,kl->sjl', left_imag, cosine_table, precision=highest) + orient * jnp.einsum('sjk,kl->sjl', left_real, sine_table, precision=highest)
    return (out_real, out_imag)

def laplace(values):
    padded = jnp.pad(values, ((0, 0), (1, 1), (1, 1)))
    neighbours = padded[:, 2:, 1:-1] + padded[:, :-2, 1:-1] + padded[:, 1:-1, 2:] + padded[:, 1:-1, :-2]
    return 4.0 * values - neighbours

def reference(spectrum, measured, pupil_mask, led_count, led_owner, led_offset):
    cosine_table, sine_table = dft_tables(B)
    pupil = pupil_mask.astype(jnp.float32)
    capture_ids = jnp.arange(CAPTURES, dtype=jnp.int32)
    slot_ids = jnp.arange(LED_MOST, dtype=jnp.int32)
    live = (slot_ids[None, :] < led_count[:, None]).astype(jnp.float32).reshape(-1)[:, None, None]
    top_rows = (capture_ids // N_TX * TILE_R)[:, None] + led_offset[:, :, 0]
    left_cols = led_owner * TILE_C + led_offset[:, :, 1]
    top_rows = top_rows.reshape(-1).astype(jnp.int32)
    left_cols = left_cols.reshape(-1).astype(jnp.int32)
    anchor = jnp.zeros((), jnp.int32)

    def extract(values):

        def one_block(row_at, col_at):
            return lax.dynamic_slice(values, (anchor, row_at, col_at), (2, B, B))
        blocks = jax.vmap(one_block)(top_rows, left_cols)
        return (blocks[:, 0] * pupil, blocks[:, 1] * pupil)
    field_real, field_imag = transform(*extract(spectrum), cosine_table, sine_table, 1.0)

    def per_capture(images):
        return lax.optimization_barrier(jnp.sum((images * live).reshape(CAPTURES, LED_MOST, B, B), axis=1))

    def forward(values):
        lin_real, lin_imag = transform(*extract(values), cosine_table, sine_table, 1.0)
        return per_capture(2.0 * (field_real * lin_real + field_imag * lin_imag))

    def adjoint(capture_imgs):
        spread = jnp.repeat(capture_imgs, LED_MOST, axis=0)
        back_real, back_imag = transform(2.0 * field_real * spread, 2.0 * field_imag * spread, cosine_table, sine_table, -1.0)
        contrib = jnp.stack([back_real * pupil * live, back_imag * pupil * live], axis=1)

        def add_block(pair_no, deposit):
            corner = (anchor, top_rows[pair_no], left_cols[pair_no])
            window = lax.dynamic_slice(deposit, corner, (2, B, B))
            return lax.dynamic_update_slice(deposit, window + contrib[pair_no], corner)
        return lax.fori_loop(0, CAPTURES * LED_MOST, add_block, jnp.zeros_like(spectrum))
    intensity = per_capture(field_real * field_real + field_imag * field_imag)
    misfit = intensity - measured
    gradient = adjoint(misfit) + REG * laplace(spectrum)

    def operator(values):
        return adjoint(forward(values)) + REG * laplace(values)
    spectrum_step = jnp.zeros_like(spectrum)
    cg_residual = -gradient
    heading = cg_residual
    res_norm = jnp.sum(cg_residual * cg_residual)
    for round_no in range(ITERS):
        applied = operator(heading)
        step_len = res_norm / jnp.sum(heading * applied)
        spectrum_step = spectrum_step + step_len * heading
        cg_residual = cg_residual - step_len * applied
        new_norm = jnp.sum(cg_residual * cg_residual)
        heading = cg_residual + new_norm / res_norm * heading
        res_norm = new_norm
    return (spectrum_step, cg_residual)
```

```python
import jax
import jax.numpy as jnp
import numpy as np
from jax import lax
from jax.experimental import pallas as pl
from jax.experimental.pallas import tpu as pltpu
from jax.sharding import PartitionSpec as P

B = 256
H = 128
T = 512
S = 8
N = 16
REG = 0.5
F32 = jnp.float32
BF = jnp.bfloat16
MESH = pl.DeviceIdType.MESH
VM = pl.BlockSpec(memory_space=pltpu.VMEM)
SM = pl.BlockSpec(memory_space=pltpu.SMEM)


def tables():
    m = np.arange(H)
    out = []
    for p in range(2):
        ang = ((2 * m[:, None] + p) * m[None, :] % B) * (2.0 * np.pi / B)
        re, im = np.cos(ang) / 16.0, np.sin(ang) / 16.0
        out.append(np.block([[re, -im], [im, re]]))
    full = np.stack([out[0], out[1], out[0].T, out[1].T])
    hi = full.astype(np.float32).astype(jnp.bfloat16)
    lo = (full - hi.astype(np.float64)).astype(np.float32).astype(jnp.bfloat16)
    return jnp.asarray(np.stack([hi, lo]))


def split(x):
    hi = x.astype(BF)
    return hi, (x - hi.astype(F32)).astype(BF)


def mm(a, b):
    return jnp.dot(a, b, preferred_element_type=F32)


def left(tab, k, x):
    hi, lo = split(x)
    return mm(tab[0, k], hi) + (mm(tab[0, k], lo) + mm(tab[1, k], hi))


def right(tab, k, x):
    hi, lo = split(x)
    return mm(hi, tab[0, k]) + (mm(lo, tab[0, k]) + mm(hi, tab[1, k]))


def masks(r, c, rows, base):
    row = lax.broadcasted_iota(jnp.int32, (rows, B), 0) + base < r
    col = lax.broadcasted_iota(jnp.int32, (rows, B), 1) < c
    return row, col


def gather(v, part, s, r, c, pup):
    halves = []
    for k1 in range(2):
        a = k1 * H
        row, col = masks(r, c, H, a)
        top = jnp.where(col, v[part, a:a + H, B:T], v[part, a:a + H, 0:B])
        bot = jnp.where(col, v[part, B + a:B + a + H, B:T], v[part, B + a:B + a + H, 0:B])
        halves.append(jnp.where(row, bot, top) * pup[s, a:a + H, :])
    return halves


def forward(v, s, r, c, pup, tab):
    re, im = gather(v, 0, s, r, c, pup), gather(v, 1, s, r, c, pup)
    rows = []
    for p in range(2):
        if p == 0:
            a = jnp.concatenate([re[0] + re[1], im[0] + im[1]], axis=0)
        else:
            a = jnp.concatenate([re[0] - re[1], im[0] - im[1]], axis=0)
        rows.append(left(tab, p, a))
    out = []
    for q in range(2):
        b = []
        for p in range(2):
            y = rows[p]
            z = y[:, :H] + y[:, H:] if q == 0 else y[:, :H] - y[:, H:]
            b.append(jnp.concatenate([z[:H], z[H:]], axis=1))
        out.append(right(tab, 2 + q, jnp.concatenate(b, axis=0)))
    return out


def backward(f, s, w, tab):
    g = []
    for q in range(2):
        wq = 2.0 * w[:, q * H:(q + 1) * H]
        g.append(right(tab, q, f[s, q] * jnp.concatenate([wq, wq], axis=1)))
    a, b = g[0] + g[1], g[0] - g[1]
    re = jnp.concatenate([a[:, :H], b[:, :H]], axis=1)
    im = jnp.concatenate([a[:, H:], b[:, H:]], axis=1)
    y = []
    for p in range(2):
        y.append(left(tab, 2 + p, jnp.concatenate([re[p * H:(p + 1) * H], im[p * H:(p + 1) * H]], axis=0)))
    plus, minus = y[0] + y[1], y[0] - y[1]
    return (plus[:H], minus[:H]), (plus[H:], minus[H:])


def deposit(out, s, r, c, pup, parts):
    for k1 in range(2):
        a = k1 * H
        row, col = masks(r, c, H, a)
        pu = pup[s, a:a + H, :]
        for part in range(2):
            x = parts[part][k1] * pu
            up, down = jnp.where(row, 0.0, x), jnp.where(row, x, 0.0)
            out[part, a:a + H, 0:B] += jnp.where(col, 0.0, up)
            out[part, a:a + H, B:T] += jnp.where(col, up, 0.0)
            out[part, B + a:B + a + H, 0:B] += jnp.where(col, 0.0, down)
            out[part, B + a:B + a + H, B:T] += jnp.where(col, down, 0.0)


def pack_edges(v, edge):
    for part in range(2):
        edge[part:part + 1, :] = v[part, 0:1, :]
        edge[2 + part:3 + part, :] = v[part, T - 1:T, :]
        edge[4 + part:5 + part, :] = jnp.transpose(v[part, :, 0:H])[0:1, :]
        edge[6 + part:7 + part, :] = jnp.transpose(v[part, :, T - H:T])[H - 1:H, :]


def laplace_to(out, get, halo, scale):
    cols = jnp.transpose(halo[...])
    row = lax.broadcasted_iota(jnp.int32, (T, T), 0)
    col = lax.broadcasted_iota(jnp.int32, (T, T), 1)
    for part in range(2):
        x = get(part)
        up = jnp.where(row == 0, halo[part:part + 1, :], pltpu.roll(x, 1, axis=0))
        down = jnp.where(row == T - 1, halo[2 + part:3 + part, :], pltpu.roll(x, T - 1, axis=0))
        lt = jnp.where(col == 0, cols[:, 4 + part:5 + part], pltpu.roll(x, 1, axis=1))
        rt = jnp.where(col == T - 1, cols[:, 6 + part:7 + part], pltpu.roll(x, T - 1, axis=1))
        out[part] = scale * (4.0 * x - ((up + down) + (lt + rt)))


def fwd0_kernel(rc, v, mask, tab, f, img, pup, edge):
    base = mask[...].astype(F32)
    pack_edges(v, edge)

    def body(s, _):
        r, c = rc[s, 0], rc[s, 1]
        rolled = pltpu.roll(pltpu.roll(base, jnp.bitwise_and(r, B - 1), axis=0), jnp.bitwise_and(c, B - 1), axis=1)
        pup[s] = rolled * rc[s, 2].astype(F32)
        z = forward(v, s, r, c, pup, tab)
        for q in range(2):
            f[s, q] = z[q]
            img[s, :, q * H:(q + 1) * H] = z[q][:, :H] * z[q][:, :H] + z[q][:, H:] * z[q][:, H:]
        return 0

    lax.fori_loop(0, S, body, 0)


def fwd_kernel(rc, v, f, pup, tab, img, edge):
    pack_edges(v, edge)

    def body(s, _):
        z = forward(v, s, rc[s, 0], rc[s, 1], pup, tab)
        for q in range(2):
            fq = f[s, q]
            img[s, :, q * H:(q + 1) * H] = 2.0 * (fq[:, :H] * z[q][:, :H] + fq[:, H:] * z[q][:, H:])
        return 0

    lax.fori_loop(0, S, body, 0)


def spread_sum(x):
    return jnp.sum(x.reshape(-1, 8, H), axis=0)


def total(a, b):
    acc = jnp.zeros((8, H), F32)
    for part in range(2):
        for i in range(0, T, 64):
            acc = acc + jnp.sum((a(part, i) * b(part, i)).reshape(8, 8, T), axis=0).reshape(8, 4, H).sum(axis=1)
    return jnp.sum(acc, axis=0, keepdims=True)


def rows_of(ref):
    return lambda part, i: ref[part, i:i + 64, :]


def adj0_kernel(rc, v, f, w, pup, tab, halo, q0):
    laplace_to(q0, lambda part: v[part], halo, -REG)

    def body(s, _):
        parts = backward(f, s, -w[s], tab)
        deposit(q0, s, rc[s, 0], rc[s, 1], pup, parts)
        return 0

    lax.fori_loop(0, S, body, 0)


def adj1_kernel(rc, v, f, w, pup, tab, halo, q1, dots):
    laplace_to(q1, lambda part: v[part], halo, REG)

    def body(s, _):
        deposit(q1, s, rc[s, 0], rc[s, 1], pup, backward(f, s, w[s], tab))
        return 0

    lax.fori_loop(0, S, body, 0)
    dots[...] = jnp.zeros((8, H), F32)
    a, b = rows_of(v), rows_of(q1)
    dots[0:1, :] = total(a, a)
    dots[1:2, :] = total(a, b)
    dots[2:3, :] = total(b, b)


def scalars(red):
    lane = jnp.sum(red[...], axis=1, keepdims=True)
    res, hah, aa = lane[0:1], lane[1:2], lane[2:3]
    alpha = res / hah
    beta = (res - 2.0 * alpha * hah + alpha * alpha * aa) / res
    return alpha, beta


def adj2_kernel(rc, red, q0, q1, f, w, pup, tab, halo0, halo1, a2, h2, dots, halo):
    alpha, beta = scalars(red)
    one = 1.0 + beta
    halo[...] = one * halo0[...] - alpha * halo1[...]
    for part in range(2):
        h2[part] = one * q0[part] - alpha * q1[part]
    laplace_to(a2, lambda part: h2[part], halo, REG)

    def body(s, _):
        deposit(a2, s, rc[s, 0], rc[s, 1], pup, backward(f, s, w[s], tab))
        return 0

    lax.fori_loop(0, S, body, 0)
    dots[...] = jnp.zeros((8, H), F32)

    def res(part, i):
        return q0[part, i:i + 64, :] - alpha * q1[part, i:i + 64, :]

    dots[0:1, :] = total(res, res)
    dots[1:2, :] = total(rows_of(h2), rows_of(a2))


def finish_kernel(red, red2, q0, q1, h2, a2, step, resid):
    alpha, _ = scalars(red)
    lane = jnp.sum(red2[...], axis=1, keepdims=True)
    alpha2 = lane[0:1] / lane[1:2]
    for part in range(2):
        step[part] = alpha * q0[part] + alpha2 * h2[part]
        resid[part] = q0[part] - alpha * q1[part] - alpha2 * a2[part]


def here():
    tx = lax.axis_index("tx")
    return tx // 4, tx % 4


def exchange_kernel(phase, slot, cap, img, edge, *rest):
    if phase == 0:
        meas, wret_o, halo_o = rest[:3]
        rest = rest[3:]
    elif phase == 1:
        wret_o, halo_o, keep = rest[:3]
        rest = rest[3:]
    else:
        red, kept, wret_o, halo_o = rest[:4]
        rest = rest[4:]
    (r1, p2, r2, wl, sb, wret, halo, sem1s, sem1r, sem2s, sem2r, sem3s, sem3r, sem4s, sem4r, hs, hr) = rest
    z, y = here()
    ty = lax.axis_index("ty")
    tx = lax.axis_index("tx")
    zd = [z if d == 0 else lax.rem(z + d, 4) for d in range(4)]
    yd = [y if d == 0 else lax.rem(y + d, 4) for d in range(4)]
    tile = [[zd[d] * 4 + y for d in range(4)], [z * 4 + yd[d] for d in range(4)]]
    across = [zd, yd]
    along = [yd, zd]
    atile = [tile[1], tile[0]]

    def tile_dev(index):
        return {"tx": index}

    edge_dev = [
        {"ty": lax.rem(ty + 7, 8)}, {"ty": lax.rem(ty + 1, 8)},
        {"tx": lax.rem(tx + 15, 16)}, {"tx": lax.rem(tx + 1, 16)},
    ]
    bar = pltpu.get_barrier_semaphore()
    for half in range(2):
        for d in range(1, 4):
            pl.semaphore_signal(bar, inc=1, device_id=tile_dev(tile[half][d]), device_id_type=MESH)
    for dev in edge_dev:
        pl.semaphore_signal(bar, inc=1, device_id=dev, device_id_type=MESH)
    pl.semaphore_wait(bar, 10)

    ecopy = []
    for i, (src, dst, dev) in enumerate([(0, 2, 0), (2, 0, 1), (4, 6, 2), (6, 4, 3)]):
        ecopy.append(pltpu.make_async_remote_copy(
            src_ref=edge.at[i], dst_ref=halo.at[dst // 2],
            send_sem=hs.at[i], recv_sem=hr.at[dst // 2], device_id=edge_dev[dev], device_id_type=MESH))
    for c in ecopy:
        c.start()

    def al(x, k):
        return pl.multiple_of(x * k, 8)

    count = S + 1 if phase == 0 else S

    def copy1(half, d, s, src):
        return pltpu.make_async_remote_copy(
            src_ref=src, dst_ref=r1.at[half, 4 - d, s], send_sem=sem1s.at[half, d, s],
            recv_sem=sem1r.at[half, 4 - d, s], device_id=tile_dev(tile[half][d]), device_id_type=MESH)

    def source(half, d, s):
        rows = pl.ds(half * H + al(across[half][d], 32), 32)
        return meas.at[rows, :] if s is None else img.at[s, rows, :]

    def send1(s, _):
        for d in (2, 1, 3):
            for half in range(2):
                copy1(half, d, s, source(half, d, s)).start()
        for half in range(2):
            rows = pl.ds(half * H + al(across[half][0], 32), 32)
            r1[half, 0, s] = img[s, rows, :]
        return 0

    lax.fori_loop(0, S, send1, 0)
    if phase == 0:
        for d in (2, 1, 3):
            for half in range(2):
                copy1(half, d, S, source(half, d, None)).start()
        for half in range(2):
            r1[half, 0, S] = meas[pl.ds(half * H + al(across[half][0], 32), 32), :]
    for half in range(2):
        for d in range(4):
            r1[half, d, S + 1] = jnp.zeros((32, B), F32)

    def wait1(s, _):
        for half in range(2):
            for d in range(1, 4):
                copy1(half, d, s, img.at[0, 0:32, :]).wait()
        return 0

    lax.fori_loop(0, count, wait1, 0)

    def partial(c, _):
        for half in range(2):
            acc = r1[half, 0, slot[tile[half][0], c]]
            for d in range(1, 4):
                acc = acc + r1[half, d, slot[tile[half][d], c]]
            p2[half, c] = acc
        return 0

    lax.fori_loop(0, N, partial, 0)
    if phase == 0:
        for half in range(2):
            for d in range(4):
                p2[half, tile[half][d]] -= r1[half, d, S]

    def copy2(half, d):
        return pltpu.make_async_remote_copy(
            src_ref=p2.at[half, :, pl.ds(al(along[half][d], 8), 8), :], dst_ref=r2.at[half, 4 - d],
            send_sem=sem2s.at[half, d], recv_sem=sem2r.at[half, 4 - d],
            device_id=tile_dev(atile[half][d]), device_id_type=MESH)

    for d in (2, 1, 3):
        for half in range(2):
            copy2(half, d).start()
    for d in (2, 1, 3):
        for half in range(2):
            copy2(half, d).wait()
    for half in range(2):
        mine = pl.ds(al(along[half][0], 8), 8)
        w = p2[half, :, mine, :] + r2[half, 1] + (r2[half, 2] + r2[half, 3])
        if phase == 1:
            keep[half] = w
        if phase == 2:
            alpha, beta = scalars(red)
            w = (1.0 + beta)[0, 0] * kept[half] - alpha[0, 0] * w
        wl[half, :, mine, :] = w

    def copy3(half, d):
        mine = pl.ds(al(along[half][0], 8), 8)
        return pltpu.make_async_remote_copy(
            src_ref=wl.at[half, :, mine, :], dst_ref=wl.at[half, :, mine, :],
            send_sem=sem3s.at[half, d], recv_sem=sem3r.at[half, 4 - d],
            device_id=tile_dev(atile[half][d]), device_id_type=MESH)

    for d in (2, 1, 3):
        for half in range(2):
            copy3(half, d).start()
    for d in (2, 1, 3):
        for half in range(2):
            c = copy3(half, d)
            c.wait_send()
            from_rows = pl.ds(al(along[half][4 - d], 8), 8)
            pltpu.make_async_remote_copy(
                src_ref=wl.at[half, :, from_rows, :], dst_ref=wl.at[half, :, from_rows, :],
                send_sem=sem3s.at[half, d], recv_sem=sem3r.at[half, 4 - d],
                device_id=tile_dev(atile[half][d]), device_id_type=MESH).wait_recv()

    def copy4(half, d, s, owner):
        rows = pl.ds(half * H + al(across[half][owner], 32), 32)
        return pltpu.make_async_remote_copy(
            src_ref=sb.at[half, d, s], dst_ref=wret.at[s, rows, :], send_sem=sem4s.at[half, d, s],
            recv_sem=sem4r.at[half, 4 - d, s], device_id=tile_dev(tile[half][d]), device_id_type=MESH)

    def send4(s, _):
        for d in (2, 1, 3):
            for half in range(2):
                sb[half, d, s] = wl[half, cap[tile[half][d], s]]
                copy4(half, d, s, 0).start()
        for half in range(2):
            rows = pl.ds(half * H + al(across[half][0], 32), 32)
            wret[s, rows, :] = wl[half, cap[tile[half][0], s]]
        return 0

    lax.fori_loop(0, S, send4, 0)

    def wait4(s, _):
        for half in range(2):
            for d in range(1, 4):
                copy4(half, d, s, 0).wait_send()
                copy4(half, d, s, 4 - d).wait_recv()
        return 0

    lax.fori_loop(0, S, wait4, 0)
    for c in ecopy:
        c.wait()

    def out(s, _):
        wret_o[s] = wret[s]
        return 0

    lax.fori_loop(0, S, out, 0)
    for i, edge_on in enumerate((ty > 0, ty < 7, tx > 0, tx < 15)):
        halo_o[i] = jnp.where(edge_on, halo[i], 0.0)


def reduce_kernel(x, out, rx, ry, mid, ss, rs, ss2, rs2):
    ty, tx = lax.axis_index("ty"), lax.axis_index("tx")
    bar = pltpu.get_barrier_semaphore()
    for d in range(1, 16):
        pl.semaphore_signal(bar, inc=1, device_id={"tx": lax.rem(tx + d, 16)}, device_id_type=MESH)
    for d in range(1, 8):
        pl.semaphore_signal(bar, inc=1, device_id={"ty": lax.rem(ty + d, 8)}, device_id_type=MESH)
    pl.semaphore_wait(bar, 22)
    copies = [pltpu.make_async_remote_copy(
        src_ref=x, dst_ref=rx.at[d], send_sem=ss.at[d], recv_sem=rs.at[d],
        device_id={"tx": lax.rem(tx + d, 16)}, device_id_type=MESH) for d in range(1, 16)]
    for c in copies:
        c.start()
    for c in copies:
        c.wait()
    acc = x[...]
    for d in range(1, 16):
        acc = acc + rx[d]
    mid[...] = acc
    copies = [pltpu.make_async_remote_copy(
        src_ref=mid, dst_ref=ry.at[d], send_sem=ss2.at[d], recv_sem=rs2.at[d],
        device_id={"ty": lax.rem(ty + d, 8)}, device_id_type=MESH) for d in range(1, 8)]
    for c in copies:
        c.start()
    for c in copies:
        c.wait()
    acc = mid[...]
    for d in range(1, 8):
        acc = acc + ry[d]
    out[...] = acc


def sds(*shape):
    return jax.ShapeDtypeStruct(shape, F32)


def call(kernel, ins, outs, scratch=(), cid=None, name=None):
    params = dict(vmem_limit_bytes=62 << 20)
    if cid is not None:
        params.update(collective_id=cid, has_side_effects=True)
    specs = [SM if x.dtype == jnp.int32 and x.shape != (B, B) else VM for x in ins]
    return pl.pallas_call(
        kernel, out_shape=outs, in_specs=specs, out_specs=[VM] * len(outs), scratch_shapes=list(scratch),
        compiler_params=pltpu.CompilerParams(**params), name=name)(*ins)


def exchange(phase, ins, outs):
    dma = pltpu.SemaphoreType.DMA
    scratch = [
        pltpu.VMEM((2, 4, S + 2, 32, B), F32), pltpu.VMEM((2, N, 32, B), F32), pltpu.VMEM((2, 4, N, 8, B), F32),
        pltpu.VMEM((2, N, 32, B), F32), pltpu.VMEM((2, 4, S, 32, B), F32), pltpu.VMEM((S, B, B), F32),
        pltpu.VMEM((4, 2, T), F32),
        dma((2, 4, S + 1)), dma((2, 4, S + 1)), dma((2, 4)), dma((2, 4)), dma((2, 4)), dma((2, 4)),
        dma((2, 4, S)), dma((2, 4, S)), dma((4,)), dma((4,)),
    ]
    return call(lambda *refs: exchange_kernel(phase, *refs), ins, outs, scratch, cid=phase, name="exchange%d" % phase)


def all_sum(x, cid):
    dma = pltpu.SemaphoreType.DMA
    scratch = [pltpu.VMEM((16, 8, H), F32), pltpu.VMEM((8, 8, H), F32), pltpu.VMEM((8, H), F32),
               dma((16,)), dma((16,)), dma((8,)), dma((8,))]
    return call(reduce_kernel, [x], [sds(8, H)], scratch, cid=cid, name="allsum%d" % cid)[0]


def routes(led_count, led_owner, led_offset):
    row = lax.axis_index("ty") * N
    column = lax.axis_index("tx")
    owner = lax.dynamic_slice_in_dim(led_owner, row, N, 0)
    count = lax.dynamic_slice_in_dim(led_count, row, N, 0)
    offset = lax.dynamic_slice_in_dim(led_offset, row, N, 0)
    slots = jnp.arange(S, dtype=jnp.int32)
    ids = jnp.arange(N, dtype=jnp.int32)
    live = slots[None, :] < count[:, None]
    hit = (owner[:, :, None] == ids[None, None, :]) & live[:, :, None]
    served = jnp.sum(hit.astype(jnp.int32), axis=1)
    rank = jnp.sum(served[None, :, :] * (ids[None, :, None] < ids[:, None, None]).astype(jnp.int32), axis=1)
    slot = jnp.where(served > 0, rank, S + 1).T
    chosen = (served[:, :, None] > 0) & (rank[:, :, None] == slots[None, None, :])
    cap = jnp.sum(jnp.where(chosen, ids[:, None, None], 0), axis=0)
    mine = lax.dynamic_slice_in_dim(chosen.astype(jnp.int32), column, 1, 1)[:, 0]
    own = lax.dynamic_slice_in_dim(hit.astype(jnp.int32), column, 1, 2)
    corner = jnp.sum(own * offset, axis=1)
    rc = jnp.sum(mine[:, :, None] * corner[:, None, :], axis=0)
    rc = jnp.concatenate([rc, jnp.sum(mine, axis=0)[:, None]], axis=1)
    return slot, cap, rc


def on_device(spectrum, measured, pupil_mask, led_count, led_owner, led_offset):
    highest = lax.Precision.HIGHEST
    slot, cap, rc = routes(led_count, led_owner, led_offset)
    tab = tables()
    pick = np.zeros((B, B), np.float32)
    for p in range(2):
        pick[p * H + np.arange(H), 2 * np.arange(H) + p] = 1.0
    pick = jnp.asarray(pick)
    meas = jnp.dot(jnp.dot(pick, measured[0], precision=highest), pick.T, precision=highest)

    f, img, pup, edge = call(fwd0_kernel, [rc, spectrum, pupil_mask, tab],
                             [sds(S, 2, B, B), sds(S, B, B), sds(S, B, B), sds(8, T)], name="fwd0")
    w, halo = exchange(0, [slot, cap, img, edge.reshape(4, 2, T), meas], [sds(S, B, B), sds(4, 2, T)])
    q0, = call(adj0_kernel, [rc, spectrum, f, w, pup, tab, halo.reshape(8, T)], [sds(2, T, T)], name="adj0")
    img, edge = call(fwd_kernel, [rc, q0, f, pup, tab], [sds(S, B, B), sds(8, T)], name="fwd1")
    w, halo0, keep = exchange(1, [slot, cap, img, edge.reshape(4, 2, T)],
                              [sds(S, B, B), sds(4, 2, T), sds(2, N, 8, B)])
    halo0 = halo0.reshape(8, T)
    q1, dots = call(adj1_kernel, [rc, q0, f, w, pup, tab, halo0], [sds(2, T, T), sds(8, H)], name="adj1")
    red = all_sum(dots, 3)
    img, edge = call(fwd_kernel, [rc, q1, f, pup, tab], [sds(S, B, B), sds(8, T)], name="fwd2")
    w, halo1 = exchange(2, [slot, cap, img, edge.reshape(4, 2, T), red, keep], [sds(S, B, B), sds(4, 2, T)])
    a2, h2, dots = call(adj2_kernel, [rc, red, q0, q1, f, w, pup, tab, halo0, halo1.reshape(8, T)],
                        [sds(2, T, T), sds(2, T, T), sds(8, H)], [pltpu.VMEM((8, T), F32)], name="adj2")
    red2 = all_sum(dots, 4)
    step, resid = call(finish_kernel, [red, red2, q0, q1, h2, a2], [sds(2, T, T), sds(2, T, T)], name="finish")
    return step, resid


def solution(mesh):
    placed = (P(None, "ty", "tx"), P(("ty", "tx"), None, None), P(), P(), P(), P())
    return jax.shard_map(
        on_device, mesh=mesh, in_specs=placed,
        out_specs=(P(None, "ty", "tx"), P(None, "ty", "tx")), check_vma=False)
```

```python
import jax
import jax.numpy as jnp
import numpy as np
from jax import lax
from jax.experimental import pallas as pl
from jax.experimental.pallas import tpu as pltpu
from jax.sharding import PartitionSpec as P

B = 256
H = 128
T = 512
S = 8
N = 16
REG = 0.5
F32 = jnp.float32
BF = jnp.bfloat16
MESH = pl.DeviceIdType.MESH
VM = pl.BlockSpec(memory_space=pltpu.VMEM)
SM = pl.BlockSpec(memory_space=pltpu.SMEM)


def tables():
    m = np.arange(H)
    out = []
    for p in range(2):
        ang = ((2 * m[:, None] + p) * m[None, :] % B) * (2.0 * np.pi / B)
        re, im = np.cos(ang) / 16.0, np.sin(ang) / 16.0
        out.append(np.block([[re, -im], [im, re]]))
    full = np.stack([out[0], out[1], out[0].T, out[1].T])
    hi = full.astype(np.float32).astype(jnp.bfloat16)
    lo = (full - hi.astype(np.float64)).astype(np.float32).astype(jnp.bfloat16)
    return jnp.asarray(np.stack([hi, lo]))


def split(x):
    hi = x.astype(BF)
    return hi, (x - hi.astype(F32)).astype(BF)


def mm(a, b):
    return jnp.dot(a, b, preferred_element_type=F32)


def left(tab, k, x):
    hi, lo = split(x)
    return mm(tab[0, k], hi) + (mm(tab[0, k], lo) + mm(tab[1, k], hi))


def right(tab, k, x):
    hi, lo = split(x)
    return mm(hi, tab[0, k]) + (mm(lo, tab[0, k]) + mm(hi, tab[1, k]))


def masks(r, c, rows, base):
    row = lax.broadcasted_iota(jnp.int32, (rows, B), 0) + base < r
    col = lax.broadcasted_iota(jnp.int32, (rows, B), 1) < c
    return row, col


def gather(v, part, s, r, c, pup):
    halves = []
    for k1 in range(2):
        a = k1 * H
        row, col = masks(r, c, H, a)
        top = jnp.where(col, v[part, a:a + H, B:T], v[part, a:a + H, 0:B])
        bot = jnp.where(col, v[part, B + a:B + a + H, B:T], v[part, B + a:B + a + H, 0:B])
        halves.append(jnp.where(row, bot, top) * pup[s, a:a + H, :])
    return halves


def forward(v, s, r, c, pup, tab):
    re, im = gather(v, 0, s, r, c, pup), gather(v, 1, s, r, c, pup)
    rows = []
    for p in range(2):
        if p == 0:
            a = jnp.concatenate([re[0] + re[1], im[0] + im[1]], axis=0)
        else:
            a = jnp.concatenate([re[0] - re[1], im[0] - im[1]], axis=0)
        rows.append(left(tab, p, a))
    out = []
    for q in range(2):
        b = []
        for p in range(2):
            y = rows[p]
            z = y[:, :H] + y[:, H:] if q == 0 else y[:, :H] - y[:, H:]
            b.append(jnp.concatenate([z[:H], z[H:]], axis=1))
        out.append(right(tab, 2 + q, jnp.concatenate(b, axis=0)))
    return out


def backward(f, s, w, tab):
    g = []
    for q in range(2):
        wq = 2.0 * w[:, q * H:(q + 1) * H]
        g.append(right(tab, q, f[s, q] * jnp.concatenate([wq, wq], axis=1)))
    a, b = g[0] + g[1], g[0] - g[1]
    re = jnp.concatenate([a[:, :H], b[:, :H]], axis=1)
    im = jnp.concatenate([a[:, H:], b[:, H:]], axis=1)
    y = []
    for p in range(2):
        y.append(left(tab, 2 + p, jnp.concatenate([re[p * H:(p + 1) * H], im[p * H:(p + 1) * H]], axis=0)))
    plus, minus = y[0] + y[1], y[0] - y[1]
    return (plus[:H], minus[:H]), (plus[H:], minus[H:])


def deposit(out, s, r, c, pup, parts):
    for k1 in range(2):
        a = k1 * H
        row, col = masks(r, c, H, a)
        pu = pup[s, a:a + H, :]
        for part in range(2):
            x = parts[part][k1] * pu
            up, down = jnp.where(row, 0.0, x), jnp.where(row, x, 0.0)
            out[part, a:a + H, 0:B] += jnp.where(col, 0.0, up)
            out[part, a:a + H, B:T] += jnp.where(col, up, 0.0)
            out[part, B + a:B + a + H, 0:B] += jnp.where(col, 0.0, down)
            out[part, B + a:B + a + H, B:T] += jnp.where(col, down, 0.0)


def pack_edges(v, edge):
    for part in range(2):
        edge[0, part:part + 1, :] = v[part, 0:1, :]
        edge[1, part:part + 1, :] = v[part, T - 1:T, :]
        edge[2, part:part + 1, :] = jnp.transpose(v[part, :, 0:H])[0:1, :]
        edge[3, part:part + 1, :] = jnp.transpose(v[part, :, T - H:T])[H - 1:H, :]


def laplace_to(out, v, halo, scale):
    row = lax.broadcasted_iota(jnp.int32, (T, T), 0)
    col = lax.broadcasted_iota(jnp.int32, (T, T), 1)
    lcol, rcol = jnp.transpose(halo[2]), jnp.transpose(halo[3])
    for part in range(2):
        x = v[part]
        up = jnp.where(row == 0, halo[0, part:part + 1, :], pltpu.roll(x, 1, axis=0))
        down = jnp.where(row == T - 1, halo[1, part:part + 1, :], pltpu.roll(x, T - 1, axis=0))
        lt = jnp.where(col == 0, lcol[:, part:part + 1], pltpu.roll(x, 1, axis=1))
        rt = jnp.where(col == T - 1, rcol[:, part:part + 1], pltpu.roll(x, T - 1, axis=1))
        out[part] = scale * (4.0 * x - ((up + down) + (lt + rt)))


def lanes(x):
    one = jnp.sum(x, axis=0, keepdims=True)
    acc = one[:, 0:H]
    for i in range(H, x.shape[1], H):
        acc = acc + one[:, i:i + H]
    return acc


def dot_rows(a, b):
    acc = jnp.zeros((1, H), F32)
    for part in range(2):
        acc = acc + lanes(a(part) * b(part))
    return acc


def whole(ref):
    return lambda part: ref[part]


def kernel(slot, cap, rc, spectrum, mask, meas, tab, step, resid,
           f, pup, img, r1, p2, r2, wl, sb, wret, keep, edge, halo, q0, q1, h2, ax, arx, ary, amid,
           sem, sem4, asem):
    tx, ty = lax.axis_index("tx"), lax.axis_index("ty")
    z, y = tx // 4, tx % 4
    zd = [z] + [lax.rem(z + d, 4) for d in range(1, 4)]
    yd = [y] + [lax.rem(y + d, 4) for d in range(1, 4)]
    tile = [[zd[d] * 4 + y for d in range(4)], [z * 4 + yd[d] for d in range(4)]]
    across, along, atile = [zd, yd], [yd, zd], [tile[1], tile[0]]
    tx_dev = [{"tx": lax.rem(tx + d, 16)} for d in range(16)]
    ty_dev = [{"ty": lax.rem(ty + d, 8)} for d in range(8)]
    edge_dev = [ty_dev[7], ty_dev[1], tx_dev[15], tx_dev[1]]

    def remote(src, dst, send, recv, dev):
        return pltpu.make_async_remote_copy(
            src_ref=src, dst_ref=dst, send_sem=send, recv_sem=recv, device_id=dev, device_id_type=MESH)

    def wait_sent(ref, s):
        remote(ref, ref, s, s, tx_dev[1]).wait_send()

    def wait_got(ref, s):
        remote(ref, ref, s, s, tx_dev[1]).wait_recv()

    def al(x, k):
        return pl.multiple_of(x * k, 8)

    def line_rows(half, d):
        return pl.ds(half * H + al(across[half][d], 32), 32)

    def sum_start(k):
        for d in range(1, 16):
            remote(ax.at[k], arx.at[k, d], asem.at[k, 0], asem.at[k, 1], tx_dev[d]).start()

    def sum_turn(k):
        wait_sent(arx.at[k, 1:16], asem.at[k, 0])
        wait_got(arx.at[k, 1:16], asem.at[k, 1])
        acc = ax[k]
        for d in range(1, 16):
            acc = acc + arx[k, d]
        amid[k] = acc
        for d in range(1, 8):
            remote(amid.at[k], ary.at[k, d], asem.at[k, 2], asem.at[k, 3], ty_dev[d]).start()

    def sum_end(k):
        wait_sent(ary.at[k, 1:8], asem.at[k, 2])
        wait_got(ary.at[k, 1:8], asem.at[k, 3])
        acc = amid[k]
        for d in range(1, 8):
            acc = acc + ary[k, d]
        return jnp.sum(acc, axis=1, keepdims=True)

    def halo_start(ph, v):
        pack_edges(v, edge.at[ph])
        for i, dst in enumerate((1, 0, 3, 2)):
            remote(edge.at[ph, i], halo.at[ph, dst], sem.at[ph, 0], sem.at[ph, 1], edge_dev[i]).start()

    def halo_end(ph):
        wait_sent(edge.at[ph], sem.at[ph, 0])
        wait_got(halo.at[ph], sem.at[ph, 1])
        for i, inside in enumerate((ty > 0, ty < 7, tx > 0, tx < 15)):
            halo[ph, i] = jnp.where(inside, halo[ph, i], 0.0)

    def send1(ph, s):
        for d in (2, 1, 3):
            for half in range(2):
                remote(img.at[s, line_rows(half, d), :], r1.at[ph, half, 4 - d, s],
                       sem.at[ph, 2], sem.at[ph, 3], {"tx": tile[half][d]}).start()
        for half in range(2):
            r1[ph, half, 0, s] = img[s, line_rows(half, 0), :]

    def sums(ph):
        wait_sent(img.at[0:6], sem.at[ph, 2])
        wait_got(r1.at[ph, :, 1:4, 0:S], sem.at[ph, 3])
        if ph == 0:
            wait_sent(r1.at[ph, :, 1:4, S], sem.at[ph, 10])
            wait_got(r1.at[ph, :, 1:4, S], sem.at[ph, 11])

        def partial(c, _):
            for half in range(2):
                acc = r1[ph, half, 0, slot[tile[half][0], c]]
                for d in range(1, 4):
                    acc = acc + r1[ph, half, d, slot[tile[half][d], c]]
                p2[half, c] = acc
            return 0

        lax.fori_loop(0, N, partial, 0)
        if ph == 0:
            for half in range(2):
                for d in range(4):
                    p2[half, tile[half][d]] -= r1[ph, half, d, S]
        for d in (2, 1, 3):
            for half in range(2):
                remote(p2.at[half, :, pl.ds(al(along[half][d], 8), 8), :], r2.at[ph, half, 4 - d],
                       sem.at[ph, 4], sem.at[ph, 5], {"tx": atile[half][d]}).start()

    def mine(half):
        return pl.ds(al(along[half][0], 8), 8)

    def sums_end(ph, fix):
        wait_sent(r2.at[ph, :, 1:4], sem.at[ph, 4])
        wait_got(r2.at[ph, :, 1:4], sem.at[ph, 5])
        for half in range(2):
            w = (p2[half, :, mine(half), :] + r2[ph, half, 1]) + (r2[ph, half, 2] + r2[ph, half, 3])
            wl[ph, half, :, mine(half), :] = fix(half, w)
        for d in (2, 1, 3):
            for half in range(2):
                part = wl.at[ph, half, :, mine(half), :]
                remote(part, part, sem.at[ph, 6], sem.at[ph, 7], {"tx": atile[half][d]}).start()

    def give_back(ph):
        wait_sent(wl.at[ph, :, :, 0:24, :], sem.at[ph, 6])
        wait_got(wl.at[ph, :, :, 0:24, :], sem.at[ph, 7])

        def send4(s, _):
            for d in (2, 1, 3):
                for half in range(2):
                    sb[half, d - 1, s] = wl[ph, half, cap[tile[half][d], s]]
                    remote(sb.at[half, d - 1, s], wret.at[ph, s, line_rows(half, 0), :],
                           sem.at[ph, 8], sem4.at[ph, s], {"tx": tile[half][d]}).start()
            for half in range(2):
                wret[ph, s, line_rows(half, 0), :] = wl[ph, half, cap[tile[half][0], s]]
            return 0

        lax.fori_loop(0, S, send4, 0)

    def adjoint(ph, out, sign):
        def body(s, _):
            wait_got(wret.at[ph, s, 0:192, :], sem4.at[ph, s])
            w = wret[ph, s]
            deposit(out, s, rc[s, 0], rc[s, 1], pup, backward(f, s, -w if sign < 0 else w, tab))
            return 0

        lax.fori_loop(0, S, body, 0)
        wait_sent(sb, sem.at[ph, 8])

    bar = pltpu.get_barrier_semaphore()
    for dev in tx_dev[1:] + ty_dev[1:]:
        pl.semaphore_signal(bar, inc=1, device_id=dev, device_id_type=MESH)
    for ph in range(3):
        for half in range(2):
            for d in range(4):
                r1[ph, half, d, S + 1] = jnp.zeros((32, B), F32)
    pl.semaphore_wait(bar, 22)

    for d in (2, 1, 3):
        for half in range(2):
            remote(meas.at[line_rows(half, d), :], r1.at[0, half, 4 - d, S],
                   sem.at[0, 10], sem.at[0, 11], {"tx": tile[half][d]}).start()
    for half in range(2):
        r1[0, half, 0, S] = meas[line_rows(half, 0), :]
    halo_start(0, spectrum)

    def fields(s, _):
        r, c = rc[s, 0], rc[s, 1]
        base = mask[...].astype(F32)
        rolled = pltpu.roll(pltpu.roll(base, jnp.bitwise_and(r, B - 1), axis=0), jnp.bitwise_and(c, B - 1), axis=1)
        pup[s] = rolled * rc[s, 2].astype(F32)
        g = forward(spectrum, s, r, c, pup, tab)
        for q in range(2):
            f[s, q] = g[q]
            img[s, :, q * H:(q + 1) * H] = g[q][:, :H] * g[q][:, :H] + g[q][:, H:] * g[q][:, H:]
        send1(0, s)
        return 0

    lax.fori_loop(0, S, fields, 0)
    halo_end(0)
    laplace_to(q0, spectrum, halo.at[0], -REG)
    sums(0)
    sums_end(0, lambda half, w: w)
    give_back(0)
    adjoint(0, q0, -1)

    def images(ph, v):
        def body(s, _):
            g = forward(v, s, rc[s, 0], rc[s, 1], pup, tab)
            for q in range(2):
                fq = f[s, q]
                img[s, :, q * H:(q + 1) * H] = 2.0 * (fq[:, :H] * g[q][:, :H] + fq[:, H:] * g[q][:, H:])
            send1(ph, s)
            return 0

        lax.fori_loop(0, S, body, 0)

    halo_start(1, q0)
    images(1, q0)
    halo_end(1)
    laplace_to(q1, q0, halo.at[1], REG)
    ax[...] = jnp.zeros((2, 8, H), F32)
    sums(1)
    ax[0, 0:1, :] = dot_rows(whole(q0), whole(q0))
    ax[0, 1:2, :] = dot_rows(whole(q0), whole(q1))

    def keep_first(half, w):
        keep[half] = w
        ax[0, 2 + half:3 + half, :] = lanes((w * w).reshape(N * 8, B))
        return w

    sums_end(1, keep_first)
    give_back(1)
    adjoint(1, q1, 1)

    halo_start(2, q1)
    images(2, q1)
    ax[0, 4:5, :] = dot_rows(whole(q1), whole(q1))
    sum_start(0)
    halo_end(2)
    sums(2)
    sum_turn(0)
    red = sum_end(0)
    res, hah, aa = red[0:1], red[1:2] + red[2:3] + red[3:4], red[4:5]
    alpha = res / hah
    beta = (res - 2.0 * alpha * hah + alpha * alpha * aa) / res
    one = 1.0 + beta
    alpha_s, one_s = alpha[0, 0], one[0, 0]

    def second(half, w):
        w = one_s * keep[half] - alpha_s * w
        ax[1, 2 + half:3 + half, :] = lanes((w * w).reshape(N * 8, B))
        return w

    sums_end(2, second)
    for part in range(2):
        h2[part] = one_s * q0[part] - alpha_s * q1[part]
        q1[part] = q0[part] - alpha_s * q1[part]
    for i in range(4):
        halo[2, i] = one_s * halo[1, i] - alpha_s * halo[2, i]
    laplace_to(resid, h2, halo.at[2], REG)
    ax[1, 0:1, :] = dot_rows(whole(q1), whole(q1))
    ax[1, 1:2, :] = dot_rows(whole(h2), whole(resid))
    sum_start(1)
    give_back(2)
    sum_turn(1)
    adjoint(2, resid, 1)
    red = sum_end(1)
    alpha2 = (red[0:1] / (red[1:2] + red[2:3] + red[3:4]))[0, 0]
    for part in range(2):
        step[part] = alpha_s * q0[part] + alpha2 * h2[part]
        resid[part] = q1[part] - alpha2 * resid[part]


def routes(led_count, led_owner, led_offset):
    row = lax.axis_index("ty") * N
    column = lax.axis_index("tx")
    owner = lax.dynamic_slice_in_dim(led_owner, row, N, 0)
    count = lax.dynamic_slice_in_dim(led_count, row, N, 0)
    offset = lax.dynamic_slice_in_dim(led_offset, row, N, 0)
    slots = jnp.arange(S, dtype=jnp.int32)
    ids = jnp.arange(N, dtype=jnp.int32)
    live = slots[None, :] < count[:, None]
    hit = (owner[:, :, None] == ids[None, None, :]) & live[:, :, None]
    served = jnp.sum(hit.astype(jnp.int32), axis=1)
    rank = jnp.sum(served[None, :, :] * (ids[None, :, None] < ids[:, None, None]).astype(jnp.int32), axis=1)
    slot = jnp.where(served > 0, rank, S + 1).T
    chosen = (served[:, :, None] > 0) & (rank[:, :, None] == slots[None, None, :])
    cap = jnp.sum(jnp.where(chosen, ids[:, None, None], 0), axis=0)
    mine = lax.dynamic_slice_in_dim(chosen.astype(jnp.int32), column, 1, 1)[:, 0]
    own = lax.dynamic_slice_in_dim(hit.astype(jnp.int32), column, 1, 2)
    corner = jnp.sum(own * offset, axis=1)
    rc = jnp.sum(mine[:, :, None] * corner[:, None, :], axis=0)
    rc = jnp.concatenate([rc, jnp.sum(mine, axis=0)[:, None]], axis=1)
    return slot, cap, rc


def on_device(spectrum, measured, pupil_mask, led_count, led_owner, led_offset):
    highest = lax.Precision.HIGHEST
    slot, cap, rc = routes(led_count, led_owner, led_offset)
    pick = np.zeros((B, B), np.float32)
    for p in range(2):
        pick[p * H + np.arange(H), 2 * np.arange(H) + p] = 1.0
    pick = jnp.asarray(pick)
    meas = jnp.dot(jnp.dot(pick, measured[0], precision=highest), pick.T, precision=highest)
    dma = pltpu.SemaphoreType.DMA
    out = jax.ShapeDtypeStruct((2, T, T), F32)

    def vm(*shape):
        return pltpu.VMEM(shape, F32)

    return pl.pallas_call(
        kernel, out_shape=(out, out), in_specs=[SM, SM, SM, VM, VM, VM, VM], out_specs=(VM, VM),
        scratch_shapes=[
            vm(S, 2, B, B), vm(S, B, B), vm(S, B, B), vm(3, 2, 4, S + 2, 32, B), vm(2, N, 32, B),
            vm(3, 2, 4, N, 8, B), vm(3, 2, N, 32, B), vm(2, 3, S, 32, B), vm(3, S, B, B), vm(2, N, 8, B),
            vm(3, 4, 2, T), vm(3, 4, 2, T), vm(2, T, T), vm(2, T, T), vm(2, T, T),
            vm(2, 8, H), vm(2, 16, 8, H), vm(2, 8, 8, H), vm(2, 8, H),
            dma((3, 12)), dma((3, S)), dma((2, 4)),
        ],
        compiler_params=pltpu.CompilerParams(collective_id=0, has_side_effects=True, vmem_limit_bytes=63 << 20),
        name="update",
    )(slot, cap, rc, spectrum, pupil_mask, meas, tables())


def solution(mesh):
    placed = (P(None, "ty", "tx"), P(("ty", "tx"), None, None), P(), P(), P(), P())
    return jax.shard_map(
        on_device, mesh=mesh, in_specs=placed,
        out_specs=(P(None, "ty", "tx"), P(None, "ty", "tx")), check_vma=False)
```

```python
import jax
import jax.numpy as jnp
import numpy as np
from jax import lax
from jax.experimental import pallas as pl
from jax.experimental.pallas import tpu as pltpu
from jax.sharding import PartitionSpec as P

B = 256
H = 128
T = 512
S = 8
N = 16
REG = 0.5
F32 = jnp.float32
BF = jnp.bfloat16
MESH = pl.DeviceIdType.MESH
LIMIT = 52 << 20
LAG = 2
LEAD = 3
VM = pl.BlockSpec(memory_space=pltpu.VMEM)


def tables():
    m = np.arange(H)
    out = []
    for p in range(2):
        ang = ((2 * m[:, None] + p) * m[None, :] % B) * (2.0 * np.pi / B)
        re, im = np.cos(ang) / 16.0, np.sin(ang) / 16.0
        out.append(np.block([[re, -im], [im, re]]))
    full = np.stack([out[0], out[1], out[0].T, out[1].T])
    hi = full.astype(np.float32).astype(jnp.bfloat16)
    lo = (full - hi.astype(np.float64)).astype(np.float32).astype(jnp.bfloat16)
    return jnp.asarray(np.stack([hi, lo]))


def split(x):
    hi = x.astype(BF)
    return hi, (x - hi.astype(F32)).astype(BF)


def mm(a, b):
    return jnp.dot(a, b, preferred_element_type=F32)


def left(tab, k, x):
    hi, lo = split(x)
    return mm(tab[0, k], hi) + (mm(tab[0, k], lo) + mm(tab[1, k], hi))


def right(tab, k, x):
    hi, lo = split(x)
    return mm(hi, tab[0, k]) + (mm(lo, tab[0, k]) + mm(hi, tab[1, k]))


def masks(r, c, rows, base):
    row = lax.broadcasted_iota(jnp.int32, (rows, B), 0) + base < r
    col = lax.broadcasted_iota(jnp.int32, (rows, B), 1) < c
    return row, col


def gather(v, part, s, r, c, pup):
    halves = []
    for k1 in range(2):
        a = k1 * H
        row, col = masks(r, c, H, a)
        top = jnp.where(col, v[part, a:a + H, B:T], v[part, a:a + H, 0:B])
        bot = jnp.where(col, v[part, B + a:B + a + H, B:T], v[part, B + a:B + a + H, 0:B])
        halves.append(jnp.where(row, bot, top) * pup[s, a:a + H, :])
    return halves


def forward(v, s, r, c, pup, tab):
    re, im = gather(v, 0, s, r, c, pup), gather(v, 1, s, r, c, pup)
    rows = []
    for p in range(2):
        if p == 0:
            a = jnp.concatenate([re[0] + re[1], im[0] + im[1]], axis=0)
        else:
            a = jnp.concatenate([re[0] - re[1], im[0] - im[1]], axis=0)
        rows.append(left(tab, p, a))
    out = []
    for q in range(2):
        b = []
        for p in range(2):
            y = rows[p]
            z = y[:, :H] + y[:, H:] if q == 0 else y[:, :H] - y[:, H:]
            b.append(jnp.concatenate([z[:H], z[H:]], axis=1))
        out.append(right(tab, 2 + q, jnp.concatenate(b, axis=0)))
    return out


def backward(f, s, w, tab):
    g = []
    for q in range(2):
        wq = w[q]
        g.append(right(tab, q, f[s, q] * jnp.concatenate([wq, wq], axis=1)))
    a, b = g[0] + g[1], g[0] - g[1]
    re = jnp.concatenate([a[:, :H], b[:, :H]], axis=1)
    im = jnp.concatenate([a[:, H:], b[:, H:]], axis=1)
    y = []
    for p in range(2):
        y.append(left(tab, 2 + p, jnp.concatenate([re[p * H:(p + 1) * H], im[p * H:(p + 1) * H]], axis=0)))
    plus, minus = y[0] + y[1], y[0] - y[1]
    return (plus[:H], minus[:H]), (plus[H:], minus[H:])


def deposit(out, s, r, c, pup, parts):
    for k1 in range(2):
        a = k1 * H
        row, col = masks(r, c, H, a)
        pu = pup[s, a:a + H, :]
        for part in range(2):
            x = parts[part][k1] * pu
            up, down = jnp.where(row, 0.0, x), jnp.where(row, x, 0.0)
            out[part, a:a + H, 0:B] += jnp.where(col, 0.0, up)
            out[part, a:a + H, B:T] += jnp.where(col, up, 0.0)
            out[part, B + a:B + a + H, 0:B] += jnp.where(col, 0.0, down)
            out[part, B + a:B + a + H, B:T] += jnp.where(col, down, 0.0)


def pack_edges(v, edge):
    for part in range(2):
        edge[0, part:part + 1, :] = v[part, 0:1, :]
        edge[1, part:part + 1, :] = v[part, T - 1:T, :]
        edge[2, part:part + 1, :] = jnp.transpose(v[part, :, 0:H])[0:1, :]
        edge[3, part:part + 1, :] = jnp.transpose(v[part, :, T - H:T])[H - 1:H, :]


def laplace_to(out, v, halo, scale):
    row = lax.broadcasted_iota(jnp.int32, (T, T), 0)
    col = lax.broadcasted_iota(jnp.int32, (T, T), 1)
    lcol, rcol = jnp.transpose(halo[2]), jnp.transpose(halo[3])
    for part in range(2):
        x = v[part]
        up = jnp.where(row == 0, halo[0, part:part + 1, :], pltpu.roll(x, 1, axis=0))
        down = jnp.where(row == T - 1, halo[1, part:part + 1, :], pltpu.roll(x, T - 1, axis=0))
        lt = jnp.where(col == 0, lcol[:, part:part + 1], pltpu.roll(x, 1, axis=1))
        rt = jnp.where(col == T - 1, rcol[:, part:part + 1], pltpu.roll(x, T - 1, axis=1))
        out[part] = scale * (4.0 * x - ((up + down) + (lt + rt)))


def lanes(x):
    one = jnp.sum(x, axis=0, keepdims=True)
    acc = one[:, 0:H]
    for i in range(H, x.shape[1], H):
        acc = acc + one[:, i:i + H]
    return acc


def dot_rows(a, b):
    acc = jnp.zeros((1, H), F32)
    for part in range(2):
        acc = acc + lanes(a(part) * b(part))
    return acc


def whole(ref):
    return lambda part: ref[part]


def prefix(x, lane):
    total = x
    for k in (1, 2, 4, 8):
        total = total + jnp.where(lane >= k, pltpu.roll(total, k, axis=1), 0)
    return total - x


def route(ty, tx, count, owner, offset, table):
    lane = lax.broadcasted_iota(jnp.int32, (N, H), 1)
    cap_id = lane - ty * N
    group = (cap_id >= 0) & (cap_id < N)
    live = lax.broadcasted_iota(jnp.int32, (S, H), 0) < count[...]
    rows = []
    for a in range(N):
        rows.append(jnp.max(jnp.where((owner[...] == a) & live, 1, 0), axis=0, keepdims=True))
    served = jnp.where(group, jnp.concatenate(rows, axis=0), 0)
    rank = prefix(served, jnp.bitwise_and(lane, N - 1))
    table[0:N] = jnp.where(served > 0, rank, S + 1)
    caps = jnp.zeros((N, H), jnp.int32)
    for k in range(S):
        at = jnp.sum(jnp.where((served > 0) & (rank == k), cap_id, 0), axis=1, keepdims=True)
        caps = jnp.where(lane == k, at, caps)
    table[N:2 * N] = caps
    hit = jnp.where((owner[...] == tx) & live, 1, 0)
    mine = lax.broadcasted_iota(jnp.int32, (N, H), 0) == tx
    own = jnp.sum(jnp.where(mine, served, 0), axis=0, keepdims=True)
    order = jnp.sum(jnp.where(mine, rank, 0), axis=0, keepdims=True)
    slot_id = lax.broadcasted_iota(jnp.int32, (S, H), 0)
    chosen = jnp.where((own > 0) & (order == slot_id), 1, 0)
    lane8 = lax.broadcasted_iota(jnp.int32, (S, H), 1)
    out = jnp.where(lane8 == 2, jnp.sum(chosen, axis=1, keepdims=True), 0)
    for k in range(2):
        corner = jnp.zeros((1, H), jnp.int32)
        for t in range(S):
            corner = corner + hit[t:t + 1] * offset[t, k:k + 1, :]
        out = jnp.where(lane8 == k, jnp.sum(chosen * corner, axis=1, keepdims=True), out)
    table[2 * N:2 * N + S] = out


def reorder(x, pick):
    def terms(v):
        hi, rest = split(v)
        rest = v - hi.astype(F32)
        mid, low = split(rest)
        return hi, mid, low

    p, pt = pick[0], pick[1]
    a, b, c = terms(x)
    y = mm(p, a) + (mm(p, b) + mm(p, c))
    a, b, c = terms(y)
    return mm(a, pt) + (mm(b, pt) + mm(c, pt))


def kernel(count, owner, offset, spectrum, mask, measured, tab, pick, step, resid,
           f, pup, img, r1a, r1b, p2, r2, wla, wlb, sb, wret, keep, edge, halo, q0, q1, h2, meas, table, tabs, ax, arx, ary, amid,
           sem, sem4, asem, lsem):
    tx, ty = lax.axis_index("tx"), lax.axis_index("ty")
    z, y = tx // 4, tx % 4
    zd = [z] + [lax.rem(z + d, 4) for d in range(1, 4)]
    yd = [y] + [lax.rem(y + d, 4) for d in range(1, 4)]
    tile = [[zd[d] * 4 + y for d in range(4)], [z * 4 + yd[d] for d in range(4)]]
    across, along, atile = [zd, yd], [yd, zd], [tile[1], tile[0]]
    r1, wl = (r1a, r1b), (wla, wlb)
    tx_dev = [{"tx": lax.rem(tx + d, 16)} for d in range(16)]
    ty_dev = [{"ty": lax.rem(ty + d, 8)} for d in range(8)]
    edge_dev = [ty_dev[7], ty_dev[1], tx_dev[15], tx_dev[1]]

    def remote(src, dst, send, recv, dev):
        return pltpu.make_async_remote_copy(
            src_ref=src, dst_ref=dst, send_sem=send, recv_sem=recv, device_id=dev, device_id_type=MESH)

    def wait_sent(ref, s):
        remote(ref, ref, s, s, tx_dev[1]).wait_send()

    def wait_got(ref, s):
        remote(ref, ref, s, s, tx_dev[1]).wait_recv()

    def al(x, k):
        return pl.multiple_of(x * k, 8)

    def line_rows(half, d):
        return pl.ds(half * H + al(across[half][d], 32), 32)

    def sum_start(k):
        for d in range(1, 16):
            remote(ax.at[k], arx.at[k, d], asem.at[k, 0], asem.at[k, 1], tx_dev[d]).start()

    def sum_turn(k):
        wait_sent(arx.at[k, 1:16], asem.at[k, 0])
        wait_got(arx.at[k, 1:16], asem.at[k, 1])
        acc = ax[k]
        for d in range(1, 16):
            acc = acc + arx[k, d]
        amid[k] = acc
        for d in range(1, 8):
            remote(amid.at[k], ary.at[k, d], asem.at[k, 2], asem.at[k, 3], ty_dev[d]).start()

    def sum_end(k):
        wait_sent(ary.at[k, 1:8], asem.at[k, 2])
        wait_got(ary.at[k, 1:8], asem.at[k, 3])
        acc = amid[k]
        for d in range(1, 8):
            acc = acc + ary[k, d]
        return jnp.sum(acc, axis=1, keepdims=True)

    def halo_start(ph, v):
        pack_edges(v, edge.at[ph])
        for i, dst in enumerate((1, 0, 3, 2)):
            remote(edge.at[ph, i], halo.at[ph, dst], sem.at[ph, 0, 0], sem.at[ph, 0, 1], edge_dev[i]).start()

    def halo_end(ph):
        wait_sent(edge.at[ph], sem.at[ph, 0, 0])
        wait_got(halo.at[ph], sem.at[ph, 0, 1])
        for i, inside in enumerate((ty > 0, ty < 7, tx > 0, tx < 15)):
            halo[ph, i] = jnp.where(inside, halo[ph, i], 0.0)

    def send1(ph, q, s):
        for d in (2, 1, 3):
            for half in range(2):
                remote(img.at[q, s, line_rows(half, d), :], r1[q].at[ph, half, 4 - d, s],
                       sem.at[ph, q, 2], sem.at[ph, q, 3], {"tx": tile[half][d]}).start()
        for half in range(2):
            r1[q][ph, half, 0, s] = img[q, s, line_rows(half, 0), :]

    def send_meas():
        for q in range(2):
            for d in (2, 1, 3):
                for half in range(2):
                    remote(meas.at[q, line_rows(half, d), :], r1[q].at[0, half, 4 - d, S],
                           sem.at[0, q, 10], sem.at[0, q, 11], {"tx": tile[half][d]}).start()
            for half in range(2):
                r1[q][0, half, 0, S] = meas[q, line_rows(half, 0), :]

    def transforms(ph, low, high, image):
        def body(s, _):
            image(s)
            send1(ph, 0, s)

            @pl.when(s >= LAG)
            def _():
                send1(ph, 1, s - LAG)

            return 0

        lax.fori_loop(low, high, body, 0)
        if high == S:
            for s in range(S - LAG, S):
                send1(ph, 1, s)

    def sums(ph, q):
        wait_sent(img.at[q, 0:6], sem.at[ph, q, 2])
        wait_got(r1[q].at[ph, :, 1:4, 0:S], sem.at[ph, q, 3])
        if ph == 0:
            wait_sent(r1[q].at[ph, :, 1:4, S], sem.at[ph, q, 10])
            wait_got(r1[q].at[ph, :, 1:4, S], sem.at[ph, q, 11])

        def partial(c, _):
            for half in range(2):
                acc = r1[q][ph, half, 0, slot_at(tile[half][0], c)]
                for d in range(1, 4):
                    acc = acc + r1[q][ph, half, d, slot_at(tile[half][d], c)]
                p2[q, half, c] = acc
            return 0

        lax.fori_loop(0, N, partial, 0, unroll=4)
        if ph == 0:
            for half in range(2):
                for d in range(4):
                    p2[q, half, tile[half][d]] -= r1[q][ph, half, d, S]
        for d in (2, 1, 3):
            for half in range(2):
                remote(p2.at[q, half, :, pl.ds(al(along[half][d], 8), 8), :], r2.at[ph, q, half, 4 - d],
                       sem.at[ph, q, 4], sem.at[ph, q, 5], {"tx": atile[half][d]}).start()

    def mine(half):
        return pl.ds(al(along[half][0], 8), 8)

    def sums_end(ph, q, fix):
        wait_sent(r2.at[ph, q, :, 1:4], sem.at[ph, q, 4])
        wait_got(r2.at[ph, q, :, 1:4], sem.at[ph, q, 5])
        for half in range(2):
            w = (p2[q, half, :, mine(half), :] + r2[ph, q, half, 1]) + (r2[ph, q, half, 2] + r2[ph, q, half, 3])
            wl[q][ph, half, :, mine(half), :] = fix(q, half, w)
        for d in (2, 1, 3):
            for half in range(2):
                part = wl[q].at[ph, half, :, mine(half), :]
                remote(part, part, sem.at[ph, q, 6], sem.at[ph, q, 7], {"tx": atile[half][d]}).start()

    def got3(ph, q):
        wait_sent(wl[q].at[ph, :, :, 0:24, :], sem.at[ph, q, 6])
        wait_got(wl[q].at[ph, :, :, 0:24, :], sem.at[ph, q, 7])

    def send4(ph, q, s):
        for d in (2, 1, 3):
            for half in range(2):
                sb[q, half, d - 1, s] = wl[q][ph, half, cap_at(tile[half][d], s)]
                remote(sb.at[q, half, d - 1, s], wret.at[ph, s, q, line_rows(half, 0), :],
                       sem.at[ph, 0, 8], sem4.at[ph, s], {"tx": tile[half][d]}).start()
        for half in range(2):
            wret[ph, s, q, line_rows(half, 0), :] = wl[q][ph, half, cap_at(tile[half][0], s)]

    def give_back(ph, between=None):
        got3(ph, 0)
        lax.fori_loop(0, LEAD, lambda s, _: (send4(ph, 0, s), 0)[1], 0)
        if between is not None:
            between()
        got3(ph, 1)
        lax.fori_loop(0, LEAD, lambda s, _: (send4(ph, 1, s), 0)[1], 0)

        def rest(s, _):
            send4(ph, 0, s)
            send4(ph, 1, s)
            return 0

        lax.fori_loop(LEAD, S, rest, 0)

    def adjoint(ph, out, sign):
        def body(s, _):
            wait_got(wret.at[ph, s, :, 0:192, :], sem4.at[ph, s])
            w = [wret[ph, s, q] * (2.0 * sign) for q in range(2)]
            r, c = corner(s)
            deposit(out, s, r, c, pup, backward(f, s, w, tab))
            return 0

        lax.fori_loop(0, S, body, 0)
        wait_sent(sb, sem.at[ph, 0, 8])

    def slot_at(a, c):
        return tabs[a, ty * N + c]

    def cap_at(a, s):
        return tabs[N + a, s]

    def corner(s):
        return tabs[2 * N + s, 0], tabs[2 * N + s, 1]

    bar = pltpu.get_barrier_semaphore()
    for dev in tx_dev[1:] + ty_dev[1:]:
        pl.semaphore_signal(bar, inc=1, device_id=dev, device_id_type=MESH)
    for ph in range(3):
        for half in range(2):
            for d in range(4):
                for q in range(2):
                    r1[q][ph, half, d, S + 1] = jnp.zeros((32, H), F32)
    route(ty, tx, count, owner, offset, table)
    to_scalar = pltpu.make_async_copy(table, tabs, lsem)
    to_scalar.start()
    ordered = reorder(measured[0], pick)
    for q in range(2):
        meas[q] = ordered[:, q * H:(q + 1) * H]
    ax[...] = jnp.zeros((2, 8, H), F32)
    to_scalar.wait()
    pl.semaphore_wait(bar, 22)

    send_meas()

    def fields(s):
        r, c = corner(s)
        base = mask[...].astype(F32)
        rolled = pltpu.roll(pltpu.roll(base, jnp.bitwise_and(r, B - 1), axis=0), jnp.bitwise_and(c, B - 1), axis=1)
        pup[s] = rolled * tabs[2 * N + s, 2].astype(F32)
        g = forward(spectrum, s, r, c, pup, tab)
        for q in range(2):
            f[s, q] = g[q]
            img[q, s] = g[q][:, :H] * g[q][:, :H] + g[q][:, H:] * g[q][:, H:]

    def image_of(v):
        def image(s):
            r, c = corner(s)
            g = forward(v, s, r, c, pup, tab)
            for q in range(2):
                fq = f[s, q]
                img[q, s] = 2.0 * (fq[:, :H] * g[q][:, :H] + fq[:, H:] * g[q][:, H:])

        return image

    transforms(0, 0, S, fields)
    halo_start(0, spectrum)
    sums(0, 0)
    sums(0, 1)
    halo_end(0)
    laplace_to(q0, spectrum, halo.at[0], -REG)
    for q in range(2):
        sums_end(0, q, lambda q, half, w: w)
    give_back(0)
    adjoint(0, q0, -1.0)

    transforms(1, 0, S, image_of(q0))
    halo_start(1, q0)
    sums(1, 0)
    sums(1, 1)
    halo_end(1)
    laplace_to(q1, q0, halo.at[1], REG)

    def keep_first(q, half, w):
        keep[q, half] = w
        k = 2 + 2 * q + half
        ax[0, k:k + 1, :] = lanes((w * w).reshape(N * 8, H))
        return w

    for q in range(2):
        sums_end(1, q, keep_first)
    ax[0, 0:1, :] = dot_rows(whole(q0), whole(q0))
    ax[0, 1:2, :] = dot_rows(whole(q0), whole(q1))
    give_back(1)
    adjoint(1, q1, 1.0)

    transforms(2, 0, 2, image_of(q1))
    ax[0, 6:7, :] = dot_rows(whole(q1), whole(q1))
    sum_start(0)
    transforms(2, 2, S, image_of(q1))
    halo_start(2, q1)
    sum_turn(0)
    sums(2, 0)
    sums(2, 1)
    red = sum_end(0)

    def heading_image(red):
        return (red[1:2] + red[2:3]) + ((red[3:4] + red[4:5]) + red[5:6])

    res, hah, aa = red[0:1], heading_image(red), red[6:7]
    alpha = res / hah
    beta = (res - 2.0 * alpha * hah + alpha * alpha * aa) / res
    alpha_s, one_s = alpha[0, 0], (1.0 + beta)[0, 0]
    halo_end(2)
    for i in range(4):
        halo[2, i] = one_s * halo[1, i] - alpha_s * halo[2, i]
    for part in range(2):
        h2[part] = one_s * q0[part] - alpha_s * q1[part]
        q1[part] = q0[part] - alpha_s * q1[part]
    laplace_to(resid, h2, halo.at[2], REG)

    def second(q, half, w):
        w = one_s * keep[q, half] - alpha_s * w
        k = 2 + 2 * q + half
        ax[1, k:k + 1, :] = lanes((w * w).reshape(N * 8, H))
        return w

    for q in range(2):
        sums_end(2, q, second)
    ax[1, 0:1, :] = dot_rows(whole(q1), whole(q1))
    ax[1, 1:2, :] = dot_rows(whole(h2), whole(resid))
    sum_start(1)
    give_back(2, lambda: sum_turn(1))
    red = sum_end(1)
    alpha2 = (red[0:1] / heading_image(red))[0, 0]
    for part in range(2):
        step[part] = alpha_s * q0[part] + alpha2 * h2[part]
        resid[part] = q1[part] - alpha2 * resid[part]
    adjoint(2, resid, -alpha2)


def on_device(spectrum, measured, pupil_mask, led_count, led_owner, led_offset):
    pick = np.zeros((B, B), np.float32)
    for p in range(2):
        pick[p * H + np.arange(H), 2 * np.arange(H) + p] = 1.0
    pick = jnp.asarray(np.stack([pick, pick.T]).astype(jnp.bfloat16))
    dma = pltpu.SemaphoreType.DMA
    out = pltpu.VMEM((2, T, T), F32)

    def vm(*shape):
        return pltpu.VMEM(shape, F32)

    return pl.pallas_call(
        kernel, out_shape=(out, out), in_specs=[VM] * 8, out_specs=(VM, VM),
        scratch_shapes=[
            vm(S, 2, B, B), vm(S, B, B), vm(2, S, B, H), vm(3, 2, 4, S + 2, 32, H), vm(3, 2, 4, S + 2, 32, H), vm(2, 2, N, 32, H),
            vm(3, 2, 2, 4, N, 8, H), vm(3, 2, N, 32, H), vm(3, 2, N, 32, H), vm(2, 2, 3, S, 32, H), vm(3, S, 2, B, H),
            vm(2, 2, N, 8, H), vm(3, 4, 2, T), vm(3, 4, 2, T), vm(2, T, T), vm(2, T, T), vm(2, T, T), vm(2, B, H),
            pltpu.VMEM((40, H), jnp.int32), pltpu.SMEM((40, H), jnp.int32),
            vm(2, 8, H), vm(2, 16, 8, H), vm(2, 8, 8, H), vm(2, 8, H),
            dma((3, 2, 12)), dma((3, S)), dma((2, 4)), dma(()),
        ],
        compiler_params=pltpu.CompilerParams(collective_id=0, has_side_effects=True, vmem_limit_bytes=LIMIT),
        name="update",
    )(led_count.reshape(1, -1), led_owner.T, led_offset.transpose(1, 2, 0), spectrum, pupil_mask, measured,
      tables(), pick)


def solution(mesh):
    placed = (P(None, "ty", "tx"), P(("ty", "tx"), None, None), P(), P(), P(), P())
    return jax.shard_map(
        on_device, mesh=mesh, in_specs=placed,
        out_specs=(P(None, "ty", "tx"), P(None, "ty", "tx")), check_vma=False)
```

```python
import jax
import jax.numpy as jnp
import numpy as np
from jax import lax
from jax.experimental import pallas as pl
from jax.experimental.pallas import tpu as pltpu
from jax.sharding import PartitionSpec as P

B = 256
H = 128
T = 512
S = 8
N = 16
REG = 0.5
F32 = jnp.float32
BF = jnp.bfloat16
MESH = pl.DeviceIdType.MESH
LIMIT = 52 << 20
ORDER = (1, 3, 2)
CUT = 4
GROUPS = ((0, 2), (2, 4), (4, 6), (6, 7), (7, 8))
VM = pl.BlockSpec(memory_space=pltpu.VMEM)
ANY = pl.BlockSpec(memory_space=pl.ANY)


def tables():
    m = np.arange(H)
    out = []
    for p in range(2):
        ang = ((2 * m[:, None] + p) * m[None, :] % B) * (2.0 * np.pi / B)
        re, im = np.cos(ang) / 16.0, np.sin(ang) / 16.0
        out.append(np.block([[re, -im], [im, re]]))
    full = np.stack([out[0], out[1], out[0].T, out[1].T])
    hi = full.astype(np.float32).astype(jnp.bfloat16)
    lo = (full - hi.astype(np.float64)).astype(np.float32).astype(jnp.bfloat16)
    return jnp.asarray(np.stack([hi, lo]))


def split(x):
    hi = x.astype(BF)
    return hi, (x - hi.astype(F32)).astype(BF)


def mm(a, b):
    return jnp.dot(a, b, preferred_element_type=F32)


def left(tab, k, x):
    hi, lo = split(x)
    return mm(tab[0, k], hi) + (mm(tab[0, k], lo) + mm(tab[1, k], hi))


def right(tab, k, x):
    hi, lo = split(x)
    return mm(hi, tab[0, k]) + (mm(lo, tab[0, k]) + mm(hi, tab[1, k]))


def masks(r, c, rows, base):
    row = lax.broadcasted_iota(jnp.int32, (rows, B), 0) + base < r
    col = lax.broadcasted_iota(jnp.int32, (rows, B), 1) < c
    return row, col


def gather(v, part, s, r, c, pup):
    halves = []
    for k1 in range(2):
        a = k1 * H
        row, col = masks(r, c, H, a)
        top = jnp.where(col, v[part, a:a + H, B:T], v[part, a:a + H, 0:B])
        bot = jnp.where(col, v[part, B + a:B + a + H, B:T], v[part, B + a:B + a + H, 0:B])
        halves.append(jnp.where(row, bot, top) * pup[s, a:a + H, :])
    return halves


def forward(v, s, r, c, pup, tab):
    re, im = gather(v, 0, s, r, c, pup), gather(v, 1, s, r, c, pup)
    rows = []
    for p in range(2):
        if p == 0:
            a = jnp.concatenate([re[0] + re[1], im[0] + im[1]], axis=0)
        else:
            a = jnp.concatenate([re[0] - re[1], im[0] - im[1]], axis=0)
        rows.append(left(tab, p, a))
    out = []
    for q in range(2):
        b = []
        for p in range(2):
            y = rows[p]
            z = y[:, :H] + y[:, H:] if q == 0 else y[:, :H] - y[:, H:]
            b.append(jnp.concatenate([z[:H], z[H:]], axis=1))
        out.append(right(tab, 2 + q, jnp.concatenate(b, axis=0)))
    return out


def backward(f, s, w, tab):
    g = []
    for q in range(2):
        wq = w[q]
        g.append(right(tab, q, f[s, q] * jnp.concatenate([wq, wq], axis=1)))
    a, b = g[0] + g[1], g[0] - g[1]
    re = jnp.concatenate([a[:, :H], b[:, :H]], axis=1)
    im = jnp.concatenate([a[:, H:], b[:, H:]], axis=1)
    y = []
    for p in range(2):
        y.append(left(tab, 2 + p, jnp.concatenate([re[p * H:(p + 1) * H], im[p * H:(p + 1) * H]], axis=0)))
    plus, minus = y[0] + y[1], y[0] - y[1]
    return (plus[:H], minus[:H]), (plus[H:], minus[H:])


def deposit(out, s, r, c, pup, parts):
    for k1 in range(2):
        a = k1 * H
        row, col = masks(r, c, H, a)
        pu = pup[s, a:a + H, :]
        for part in range(2):
            x = parts[part][k1] * pu
            up, down = jnp.where(row, 0.0, x), jnp.where(row, x, 0.0)
            out[part, a:a + H, 0:B] += jnp.where(col, 0.0, up)
            out[part, a:a + H, B:T] += jnp.where(col, up, 0.0)
            out[part, B + a:B + a + H, 0:B] += jnp.where(col, 0.0, down)
            out[part, B + a:B + a + H, B:T] += jnp.where(col, down, 0.0)


def pack_edges(v, edge):
    for part in range(2):
        edge[0, part:part + 1, :] = v[part, 0:1, :]
        edge[1, part:part + 1, :] = v[part, T - 1:T, :]
        edge[2, part:part + 1, :] = jnp.transpose(v[part, :, 0:H])[0:1, :]
        edge[3, part:part + 1, :] = jnp.transpose(v[part, :, T - H:T])[H - 1:H, :]


def laplace_to(out, v, halo, scale):
    row = lax.broadcasted_iota(jnp.int32, (T, T), 0)
    col = lax.broadcasted_iota(jnp.int32, (T, T), 1)
    lcol, rcol = jnp.transpose(halo[2]), jnp.transpose(halo[3])
    for part in range(2):
        x = v[part]
        up = jnp.where(row == 0, halo[0, part:part + 1, :], pltpu.roll(x, 1, axis=0))
        down = jnp.where(row == T - 1, halo[1, part:part + 1, :], pltpu.roll(x, T - 1, axis=0))
        lt = jnp.where(col == 0, lcol[:, part:part + 1], pltpu.roll(x, 1, axis=1))
        rt = jnp.where(col == T - 1, rcol[:, part:part + 1], pltpu.roll(x, T - 1, axis=1))
        out[part] = scale * (4.0 * x - ((up + down) + (lt + rt)))


def lanes(x):
    one = jnp.sum(x, axis=0, keepdims=True)
    acc = one[:, 0:H]
    for i in range(H, x.shape[1], H):
        acc = acc + one[:, i:i + H]
    return acc


def dot_rows(a, b):
    acc = jnp.zeros((1, H), F32)
    for part in range(2):
        acc = acc + lanes(a(part) * b(part))
    return acc


def whole(ref):
    return lambda part: ref[part]


def prefix(x, lane):
    total = x
    for k in (1, 2, 4, 8):
        total = total + jnp.where(lane >= k, pltpu.roll(total, k, axis=1), 0)
    return total - x


def route(ty, tx, count, owner, offset, table):
    lane = lax.broadcasted_iota(jnp.int32, (N, H), 1)
    cap_id = lane - ty * N
    group = (cap_id >= 0) & (cap_id < N)
    live = lax.broadcasted_iota(jnp.int32, (S, H), 0) < count[...]
    rows = []
    for a in range(N):
        rows.append(jnp.max(jnp.where((owner[...] == a) & live, 1, 0), axis=0, keepdims=True))
    served = jnp.where(group, jnp.concatenate(rows, axis=0), 0)
    rank = prefix(served, jnp.bitwise_and(lane, N - 1))
    table[0:N] = jnp.where(served > 0, rank, S + 1)
    caps = jnp.zeros((N, H), jnp.int32)
    for k in range(S):
        at = jnp.sum(jnp.where((served > 0) & (rank == k), cap_id, 0), axis=1, keepdims=True)
        caps = jnp.where(lane == k, at, caps)
    table[N:2 * N] = caps
    hit = jnp.where((owner[...] == tx) & live, 1, 0)
    mine = lax.broadcasted_iota(jnp.int32, (N, H), 0) == tx
    own = jnp.sum(jnp.where(mine, served, 0), axis=0, keepdims=True)
    order = jnp.sum(jnp.where(mine, rank, 0), axis=0, keepdims=True)
    slot_id = lax.broadcasted_iota(jnp.int32, (S, H), 0)
    chosen = jnp.where((own > 0) & (order == slot_id), 1, 0)
    lane8 = lax.broadcasted_iota(jnp.int32, (S, H), 1)
    out = jnp.where(lane8 == 2, jnp.sum(chosen, axis=1, keepdims=True), 0)
    for k in range(2):
        corner = jnp.zeros((1, H), jnp.int32)
        for t in range(S):
            corner = corner + hit[t:t + 1] * offset[t, k:k + 1, :]
        out = jnp.where(lane8 == k, jnp.sum(chosen * corner, axis=1, keepdims=True), out)
    table[2 * N:2 * N + S] = out


def reorder(x, pick):
    def terms(v):
        hi, rest = split(v)
        rest = v - hi.astype(F32)
        mid, low = split(rest)
        return hi, mid, low

    p, pt = pick[0], pick[1]
    a, b, c = terms(x)
    y = mm(p, a) + (mm(p, b) + mm(p, c))
    a, b, c = terms(y)
    return mm(a, pt) + (mm(b, pt) + mm(c, pt))


def kernel(count, owner, offset, given, mask, measured, tab_in, pick, step, resid,
           f, pup, img, r1a, r1b, p2, r2, wla, wlb, sb, wret, keep, edge, halo, q0, q1, h2, meas, back, spectrum, tab, last, table, tabs, ax, arx, ary, amid,
           sem, sem4, asem, lsem):
    tx, ty = lax.axis_index("tx"), lax.axis_index("ty")
    z, y = tx // 4, tx % 4
    zd = [z] + [lax.rem(z + d, 4) for d in range(1, 4)]
    yd = [y] + [lax.rem(y + d, 4) for d in range(1, 4)]
    tile = [[zd[d] * 4 + y for d in range(4)], [z * 4 + yd[d] for d in range(4)]]
    across, along, atile = [zd, yd], [yd, zd], [tile[1], tile[0]]
    r1, wl = (r1a, r1b), (wla, wlb)
    tx_dev = [{"tx": lax.rem(tx + d, 16)} for d in range(16)]
    ty_dev = [{"ty": lax.rem(ty + d, 8)} for d in range(8)]
    edge_dev = [ty_dev[7], ty_dev[1], tx_dev[15], tx_dev[1]]

    def remote(src, dst, send, recv, dev):
        return pltpu.make_async_remote_copy(
            src_ref=src, dst_ref=dst, send_sem=send, recv_sem=recv, device_id=dev, device_id_type=MESH)

    def wait_sent(ref, s):
        remote(ref, ref, s, s, tx_dev[1]).wait_send()

    def wait_got(ref, s):
        remote(ref, ref, s, s, tx_dev[1]).wait_recv()

    def al(x, k):
        return pl.multiple_of(x * k, 8)

    def line_rows(half, d):
        return pl.ds(half * H + al(across[half][d], 32), 32)

    def sum_start(k):
        for d in range(1, 16):
            remote(ax.at[k], arx.at[k, d], asem.at[k, 0], asem.at[k, 1], tx_dev[d]).start()

    def sum_turn(k):
        wait_sent(arx.at[k, 1:16], asem.at[k, 0])
        wait_got(arx.at[k, 1:16], asem.at[k, 1])
        acc = ax[k]
        for d in range(1, 16):
            acc = acc + arx[k, d]
        amid[k] = acc
        for d in range(1, 8):
            remote(amid.at[k], ary.at[k, d], asem.at[k, 2], asem.at[k, 3], ty_dev[d]).start()

    def sum_end(k):
        wait_sent(ary.at[k, 1:8], asem.at[k, 2])
        wait_got(ary.at[k, 1:8], asem.at[k, 3])
        acc = amid[k]
        for d in range(1, 8):
            acc = acc + ary[k, d]
        return jnp.sum(acc, axis=1, keepdims=True)

    def halo_start(ph, v):
        pack_edges(v, edge.at[ph])
        for i, dst in enumerate((1, 0, 3, 2)):
            remote(edge.at[ph, i], halo.at[ph, dst], sem.at[ph, 0, 0], sem.at[ph, 0, 1], edge_dev[i]).start()

    def halo_end(ph):
        wait_sent(edge.at[ph], sem.at[ph, 0, 0])
        wait_got(halo.at[ph], sem.at[ph, 0, 1])
        for i, inside in enumerate((ty > 0, ty < 7, tx > 0, tx < 15)):
            halo[ph, i] = jnp.where(inside, halo[ph, i], 0.0)

    def send1(ph, q, low, count):
        if count == 1:
            src, dst = lambda rows: img.at[q, low, rows, :], lambda half, d: r1[q].at[ph, half, 4 - d, low]
        else:
            part = pl.ds(low, count)
            src, dst = lambda rows: img.at[q, part, rows, :], lambda half, d: r1[q].at[ph, half, 4 - d, part]
        for d in ORDER:
            for half in range(2):
                remote(src(line_rows(half, d)), dst(half, d), sem.at[ph, q, 2], sem.at[ph, q, 3],
                       {"tx": tile[half][d]}).start()

    def keep_own(ph, s):
        for q in range(2):
            for half in range(2):
                r1[q][ph, half, 0, s] = img[q, s, line_rows(half, 0), :]

    def send_meas():
        for q in range(2):
            for d in ORDER:
                for half in range(2):
                    remote(meas.at[q, line_rows(half, d), :], r1[q].at[0, half, 4 - d, S],
                           sem.at[0, q, 10], sem.at[0, q, 11], {"tx": tile[half][d]}).start()
            for half in range(2):
                r1[q][0, half, 0, S] = meas[q, line_rows(half, 0), :]

    def transforms(ph, low, high, image, turn=None):
        def body(s, _):
            image(s)
            send1(ph, 0, s, 1)

            @pl.when(s == CUT - 1)
            def _():
                send1(ph, 1, 0, CUT)

            keep_own(ph, s)
            if turn is not None:
                pl.when(s == 5)(turn)
            return 0

        lax.fori_loop(low, high, body, 0)
        if high == S:
            send1(ph, 1, CUT, S - CUT)

    def sums(ph, q):
        wait_sent(img.at[q, 0:6], sem.at[ph, q, 2])
        wait_got(r1[q].at[ph, :, 1:4, 0:S], sem.at[ph, q, 3])
        if ph == 0:
            wait_sent(r1[q].at[ph, :, 1:4, S], sem.at[ph, q, 10])
            wait_got(r1[q].at[ph, :, 1:4, S], sem.at[ph, q, 11])

        def partial(c, _):
            for half in range(2):
                acc = r1[q][ph, half, 0, slot_at(tile[half][0], c)]
                for d in range(1, 4):
                    acc = acc + r1[q][ph, half, d, slot_at(tile[half][d], c)]
                p2[q, half, :, c] = acc.reshape(4, 8, H)
            return 0

        lax.fori_loop(0, N, partial, 0, unroll=4)
        if ph == 0:
            for half in range(2):
                for d in range(4):
                    p2[q, half, :, tile[half][d]] -= r1[q][ph, half, d, S].reshape(4, 8, H)
        for d in ORDER:
            for half in range(2):
                remote(p2.at[q, half, along[half][d]], r2.at[ph, q, half, 4 - d],
                       sem.at[ph, q, 4], sem.at[ph, q, 5], {"tx": atile[half][d]}).start()

    def sums_end(ph, q, fix):
        wait_sent(r2.at[ph, q, :, 1:4], sem.at[ph, q, 4])
        wait_got(r2.at[ph, q, :, 1:4], sem.at[ph, q, 5])
        for half in range(2):
            w = (p2[q, half, along[half][0]] + r2[ph, q, half, 1]) + (r2[ph, q, half, 2] + r2[ph, q, half, 3])
            wl[q][ph, half, along[half][0]] = fix(q, half, w)
        for d in ORDER:
            for half in range(2):
                part = wl[q].at[ph, half, along[half][0]]
                remote(part, part, sem.at[ph, q, 6], sem.at[ph, q, 7], {"tx": atile[half][d]}).start()

    def got3(ph, q):
        wait_sent(wl[q].at[ph, :, 0:3], sem.at[ph, q, 6])
        wait_got(wl[q].at[ph, :, 0:3], sem.at[ph, q, 7])

    def stage4(ph, q, low, high):
        for s in range(low, high):
            for half in range(2):
                for d in range(4):
                    piece = wl[q][ph, half, :, cap_at(tile[half][d], s)].reshape(32, H)
                    if d == 0:
                        wret[ph, s, q, line_rows(half, 0), :] = piece
                    else:
                        sb[half, d - 1, s, q] = piece

    def send4(ph, q, g):
        low, high = GROUPS[g]
        for d in ORDER:
            for half in range(2):
                if q is None:
                    src, dst = sb.at[half, d - 1, low:high], wret.at[ph, low:high, :, line_rows(half, 0), :]
                else:
                    src, dst = sb.at[half, d - 1, low:high, q], wret.at[ph, low:high, q, line_rows(half, 0), :]
                remote(src, dst, sem.at[ph, 0, 8], sem4.at[ph, g], {"tx": tile[half][d]}).start()

    def give_back(ph):
        got3(ph, 0)
        stage4(ph, 0, *GROUPS[0])
        send4(ph, 0, 0)
        got3(ph, 1)
        stage4(ph, 1, *GROUPS[0])
        send4(ph, 1, 0)
        for g in range(1, len(GROUPS)):
            for q in range(2):
                stage4(ph, q, *GROUPS[g])
            send4(ph, None, g)

    def adjoint(ph, out, sign, late=None):
        back[1] = jnp.zeros((2, B, B), F32)

        def add_in(s, which):
            r, c = corner(s)
            deposit(out, s, r, c, pup, [[back[which, part, k * H:(k + 1) * H, :] for k in range(2)] for part in range(2)])

        def body(s, _):
            for g, (low, high) in enumerate(GROUPS):
                @pl.when(s == low)
                def _():
                    wait_got(wret.at[ph, low:high, :, 0:192, :], sem4.at[ph, g])

            if late is not None:
                pl.when(s == 5)(late)
            odd = lax.rem(s, 2)
            add_in(jnp.maximum(s - 1, 0), 1 - odd)
            w = [wret[ph, s, q] * (2.0 * sign) for q in range(2)]
            parts = backward(f, s, w, tab)
            for part in range(2):
                for k in range(2):
                    back[odd, part, k * H:(k + 1) * H, :] = parts[part][k]
            return 0

        lax.fori_loop(0, S, body, 0)
        add_in(S - 1, (S - 1) % 2)
        wait_sent(sb, sem.at[ph, 0, 8])

    def slot_at(a, c):
        return tabs[a, ty * N + c]

    def cap_at(a, s):
        return tabs[N + a, s]

    def corner(s):
        return tabs[2 * N + s, 0], tabs[2 * N + s, 1]

    bar = pltpu.get_barrier_semaphore()
    for dev in tx_dev[1:] + ty_dev[1:]:
        pl.semaphore_signal(bar, inc=1, device_id=dev, device_id_type=MESH)
    loads = [pltpu.make_async_copy(given, spectrum, lsem.at[1]), pltpu.make_async_copy(tab_in, tab, lsem.at[2])]
    for copy in loads:
        copy.start()
    for ph in range(3):
        for half in range(2):
            for d in range(4):
                for q in range(2):
                    r1[q][ph, half, d, S + 1] = jnp.zeros((32, H), F32)
    route(ty, tx, count, owner, offset, table)
    to_scalar = pltpu.make_async_copy(table, tabs, lsem.at[0])
    to_scalar.start()
    ordered = reorder(measured[0], pick)
    for q in range(2):
        meas[q] = ordered[:, q * H:(q + 1) * H]
    ax[...] = jnp.zeros((2, 8, H), F32)
    for copy in [to_scalar] + loads:
        copy.wait()

    def fields(s):
        r, c = corner(s)
        base = mask[...].astype(F32)
        rolled = pltpu.roll(pltpu.roll(base, jnp.bitwise_and(r, B - 1), axis=0), jnp.bitwise_and(c, B - 1), axis=1)
        pup[s] = rolled * tabs[2 * N + s, 2].astype(F32)
        g = forward(spectrum, s, r, c, pup, tab)
        for q in range(2):
            f[s, q] = g[q]
            img[q, s] = g[q][:, :H] * g[q][:, :H] + g[q][:, H:] * g[q][:, H:]

    def image_of(v):
        def image(s):
            r, c = corner(s)
            g = forward(v, s, r, c, pup, tab)
            for q in range(2):
                fq = f[s, q]
                img[q, s] = 2.0 * (fq[:, :H] * g[q][:, :H] + fq[:, H:] * g[q][:, H:])

        return image

    fields(0)
    pl.semaphore_wait(bar, 22)
    send_meas()
    send1(0, 0, 0, 1)
    keep_own(0, 0)
    transforms(0, 1, S, fields)
    halo_start(0, spectrum)
    sums(0, 0)
    sums(0, 1)
    halo_end(0)
    laplace_to(q0, spectrum, halo.at[0], -REG)
    for q in range(2):
        sums_end(0, q, lambda q, half, w: w)
    give_back(0)
    adjoint(0, q0, -1.0)

    transforms(1, 0, S, image_of(q0))
    halo_start(1, q0)
    sums(1, 0)
    sums(1, 1)
    halo_end(1)
    laplace_to(q1, q0, halo.at[1], REG)

    def keep_first(q, half, w):
        keep[q, half] = w
        k = 2 + 2 * q + half
        ax[0, k:k + 1, :] = lanes((w * w).reshape(N * 8, H))
        return w

    for q in range(2):
        sums_end(1, q, keep_first)
    ax[0, 0:1, :] = dot_rows(whole(q0), whole(q0))
    ax[0, 1:2, :] = dot_rows(whole(q0), whole(q1))
    give_back(1)
    adjoint(1, q1, 1.0)

    transforms(2, 0, 2, image_of(q1))
    ax[0, 6:7, :] = dot_rows(whole(q1), whole(q1))
    sum_start(0)
    transforms(2, 2, S, image_of(q1), lambda: sum_turn(0))
    halo_start(2, q1)
    sums(2, 0)
    sums(2, 1)
    red = sum_end(0)

    def heading_image(red):
        return (red[1:2] + red[2:3]) + ((red[3:4] + red[4:5]) + red[5:6])

    res, hah, aa = red[0:1], heading_image(red), red[6:7]
    alpha = res / hah
    beta = (res - 2.0 * alpha * hah + alpha * alpha * aa) / res
    alpha_s, one_s = alpha[0, 0], (1.0 + beta)[0, 0]
    halo_end(2)
    for i in range(4):
        halo[2, i] = one_s * halo[1, i] - alpha_s * halo[2, i]
    for part in range(2):
        h2[part] = one_s * q0[part] - alpha_s * q1[part]
        q1[part] = q0[part] - alpha_s * q1[part]
    laplace_to(resid, h2, halo.at[2], REG)

    def second(q, half, w):
        w = one_s * keep[q, half] - alpha_s * w
        k = 2 + 2 * q + half
        ax[1, k:k + 1, :] = lanes((w * w).reshape(N * 8, H))
        return w

    for q in range(2):
        sums_end(2, q, second)
    ax[1, 0:1, :] = dot_rows(whole(q1), whole(q1))
    ax[1, 1:2, :] = dot_rows(whole(h2), whole(resid))
    sum_start(1)
    give_back(2)
    sum_turn(1)

    def close_step():
        red = sum_end(1)
        ratio = red[0:1] / heading_image(red)
        last[...] = jnp.broadcast_to(ratio, (1, H))
        a = ratio[0, 0]
        for part in range(2):
            step[part] = alpha_s * q0[part] + a * h2[part]

    adjoint(2, resid, 1.0, close_step)
    a = last[0:1, 0:1][0, 0]
    for part in range(2):
        resid[part] = q1[part] - a * resid[part]


def on_device(spectrum, measured, pupil_mask, led_count, led_owner, led_offset):
    pick = np.zeros((B, B), np.float32)
    for p in range(2):
        pick[p * H + np.arange(H), 2 * np.arange(H) + p] = 1.0
    pick = jnp.asarray(np.stack([pick, pick.T]).astype(jnp.bfloat16))
    dma = pltpu.SemaphoreType.DMA
    out = pltpu.VMEM((2, T, T), F32)

    def vm(*shape):
        return pltpu.VMEM(shape, F32)

    return pl.pallas_call(
        kernel, out_shape=(out, out), in_specs=[VM, VM, VM, ANY, VM, VM, ANY, VM], out_specs=(VM, VM),
        scratch_shapes=[
            vm(S, 2, B, B), vm(S, B, B), vm(2, S, B, H), vm(3, 2, 4, S + 2, 32, H), vm(3, 2, 4, S + 2, 32, H), vm(2, 2, 4, N, 8, H),
            vm(3, 2, 2, 4, N, 8, H), vm(3, 2, 4, N, 8, H), vm(3, 2, 4, N, 8, H), vm(2, 3, S, 2, 32, H), vm(3, S, 2, B, H),
            vm(2, 2, N, 8, H), vm(3, 4, 2, T), vm(3, 4, 2, T), vm(2, T, T), vm(2, T, T), vm(2, T, T), vm(2, B, H), vm(2, 2, B, B), vm(2, T, T), pltpu.VMEM((2, 4, B, B), BF), vm(1, H),
            pltpu.VMEM((40, H), jnp.int32), pltpu.SMEM((40, H), jnp.int32),
            vm(2, 8, H), vm(2, 16, 8, H), vm(2, 8, 8, H), vm(2, 8, H),
            dma((3, 2, 12)), dma((3, len(GROUPS))), dma((2, 4)), dma((3,)),
        ],
        compiler_params=pltpu.CompilerParams(collective_id=0, has_side_effects=True, vmem_limit_bytes=LIMIT),
        name="update",
    )(led_count.reshape(1, -1), led_owner.T, led_offset.transpose(1, 2, 0), spectrum, pupil_mask, measured,
      tables(), pick)


def solution(mesh):
    placed = (P(None, "ty", "tx"), P(("ty", "tx"), None, None), P(), P(), P(), P())
    return jax.shard_map(
        on_device, mesh=mesh, in_specs=placed,
        out_specs=(P(None, "ty", "tx"), P(None, "ty", "tx")), check_vma=False)
```

```python
import jax
import jax.numpy as jnp
import numpy as np
from jax import lax
from jax.experimental import pallas as pl
from jax.experimental.pallas import tpu as pltpu
from jax.sharding import PartitionSpec as P

B = 256
H = 128
T = 512
S = 8
N = 16
REG = 0.5
F32 = jnp.float32
BF = jnp.bfloat16
MESH = pl.DeviceIdType.MESH
LIMIT = 52 << 20
ORDER = (1, 3, 2)
CUT = 4
GROUPS = ((0, 2), (2, 4), (4, 6), (6, 7), (7, 8))
VM = pl.BlockSpec(memory_space=pltpu.VMEM)
ANY = pl.BlockSpec(memory_space=pl.ANY)


def tables():
    m = np.arange(H)
    out = []
    for p in range(2):
        ang = ((2 * m[:, None] + p) * m[None, :] % B) * (2.0 * np.pi / B)
        re, im = np.cos(ang) / 16.0, np.sin(ang) / 16.0
        out.append(np.block([[re, -im], [im, re]]))
    full = np.stack([out[0], out[1], out[0].T, out[1].T])
    hi = full.astype(np.float32).astype(jnp.bfloat16)
    lo = (full - hi.astype(np.float64)).astype(np.float32).astype(jnp.bfloat16)
    return jnp.asarray(np.stack([hi, lo]))


def split(x):
    hi = x.astype(BF)
    return hi, (x - hi.astype(F32)).astype(BF)


def mm(a, b):
    return jnp.dot(a, b, preferred_element_type=F32)


def left(tab, k, x):
    hi, lo = split(x)
    return mm(tab[0, k], hi) + (mm(tab[0, k], lo) + mm(tab[1, k], hi))


def right(tab, k, x):
    hi, lo = split(x)
    return mm(hi, tab[0, k]) + (mm(lo, tab[0, k]) + mm(hi, tab[1, k]))


def masks(r, c, rows, base):
    row = lax.broadcasted_iota(jnp.int32, (rows, B), 0) + base < r
    col = lax.broadcasted_iota(jnp.int32, (rows, B), 1) < c
    return row, col


def gather(v, part, s, r, c, pup):
    halves = []
    for k1 in range(2):
        a = k1 * H
        row, col = masks(r, c, H, a)
        top = jnp.where(col, v[part, a:a + H, B:T], v[part, a:a + H, 0:B])
        bot = jnp.where(col, v[part, B + a:B + a + H, B:T], v[part, B + a:B + a + H, 0:B])
        halves.append(jnp.where(row, bot, top) * pup[s, a:a + H, :])
    return halves


def forward(v, s, r, c, pup, tab):
    re, im = gather(v, 0, s, r, c, pup), gather(v, 1, s, r, c, pup)
    rows = []
    for p in range(2):
        if p == 0:
            a = jnp.concatenate([re[0] + re[1], im[0] + im[1]], axis=0)
        else:
            a = jnp.concatenate([re[0] - re[1], im[0] - im[1]], axis=0)
        rows.append(left(tab, p, a))
    out = []
    for q in range(2):
        b = []
        for p in range(2):
            y = rows[p]
            z = y[:, :H] + y[:, H:] if q == 0 else y[:, :H] - y[:, H:]
            b.append(jnp.concatenate([z[:H], z[H:]], axis=1))
        out.append(right(tab, 2 + q, jnp.concatenate(b, axis=0)))
    return out


def backward(f, s, w, tab):
    g = []
    for q in range(2):
        wq = w[q]
        g.append(right(tab, q, f[s, q] * jnp.concatenate([wq, wq], axis=1)))
    a, b = g[0] + g[1], g[0] - g[1]
    re = jnp.concatenate([a[:, :H], b[:, :H]], axis=1)
    im = jnp.concatenate([a[:, H:], b[:, H:]], axis=1)
    y = []
    for p in range(2):
        y.append(left(tab, 2 + p, jnp.concatenate([re[p * H:(p + 1) * H], im[p * H:(p + 1) * H]], axis=0)))
    plus, minus = y[0] + y[1], y[0] - y[1]
    return (plus[:H], minus[:H]), (plus[H:], minus[H:])


def deposit(out, s, r, c, pup, parts):
    for k1 in range(2):
        a = k1 * H
        row, col = masks(r, c, H, a)
        pu = pup[s, a:a + H, :]
        for part in range(2):
            x = parts[part][k1] * pu
            up, down = jnp.where(row, 0.0, x), jnp.where(row, x, 0.0)
            out[part, a:a + H, 0:B] += jnp.where(col, 0.0, up)
            out[part, a:a + H, B:T] += jnp.where(col, up, 0.0)
            out[part, B + a:B + a + H, 0:B] += jnp.where(col, 0.0, down)
            out[part, B + a:B + a + H, B:T] += jnp.where(col, down, 0.0)


def pack_edges(v, edge):
    for part in range(2):
        edge[0, part:part + 1, :] = v[part, 0:1, :]
        edge[1, part:part + 1, :] = v[part, T - 1:T, :]
        edge[2, part:part + 1, :] = jnp.transpose(v[part, :, 0:H])[0:1, :]
        edge[3, part:part + 1, :] = jnp.transpose(v[part, :, T - H:T])[H - 1:H, :]


def laplace_to(out, v, halo, scale):
    row = lax.broadcasted_iota(jnp.int32, (T, T), 0)
    col = lax.broadcasted_iota(jnp.int32, (T, T), 1)
    lcol, rcol = jnp.transpose(halo[2]), jnp.transpose(halo[3])
    for part in range(2):
        x = v[part]
        up = jnp.where(row == 0, halo[0, part:part + 1, :], pltpu.roll(x, 1, axis=0))
        down = jnp.where(row == T - 1, halo[1, part:part + 1, :], pltpu.roll(x, T - 1, axis=0))
        lt = jnp.where(col == 0, lcol[:, part:part + 1], pltpu.roll(x, 1, axis=1))
        rt = jnp.where(col == T - 1, rcol[:, part:part + 1], pltpu.roll(x, T - 1, axis=1))
        out[part] = scale * (4.0 * x - ((up + down) + (lt + rt)))


def lanes(x):
    one = jnp.sum(x, axis=0, keepdims=True)
    acc = one[:, 0:H]
    for i in range(H, x.shape[1], H):
        acc = acc + one[:, i:i + H]
    return acc


def dot_rows(a, b):
    acc = jnp.zeros((1, H), F32)
    for part in range(2):
        acc = acc + lanes(a(part) * b(part))
    return acc


def whole(ref):
    return lambda part: ref[part]


def prefix(x, lane):
    total = x
    for k in (1, 2, 4, 8):
        total = total + jnp.where(lane >= k, pltpu.roll(total, k, axis=1), 0)
    return total - x


def route(ty, tx, count, owner, offset, table):
    lane = lax.broadcasted_iota(jnp.int32, (N, H), 1)
    cap_id = lane - ty * N
    group = (cap_id >= 0) & (cap_id < N)
    live = lax.broadcasted_iota(jnp.int32, (S, H), 0) < count[...]
    rows = []
    for a in range(N):
        rows.append(jnp.max(jnp.where((owner[...] == a) & live, 1, 0), axis=0, keepdims=True))
    served = jnp.where(group, jnp.concatenate(rows, axis=0), 0)
    rank = prefix(served, jnp.bitwise_and(lane, N - 1))
    table[0:N] = jnp.where(served > 0, rank, S + 1)
    caps = jnp.zeros((N, H), jnp.int32)
    for k in range(S):
        at = jnp.sum(jnp.where((served > 0) & (rank == k), cap_id, 0), axis=1, keepdims=True)
        caps = jnp.where(lane == k, at, caps)
    table[N:2 * N] = caps
    hit = jnp.where((owner[...] == tx) & live, 1, 0)
    mine = lax.broadcasted_iota(jnp.int32, (N, H), 0) == tx
    own = jnp.sum(jnp.where(mine, served, 0), axis=0, keepdims=True)
    order = jnp.sum(jnp.where(mine, rank, 0), axis=0, keepdims=True)
    slot_id = lax.broadcasted_iota(jnp.int32, (S, H), 0)
    chosen = jnp.where((own > 0) & (order == slot_id), 1, 0)
    lane8 = lax.broadcasted_iota(jnp.int32, (S, H), 1)
    out = jnp.where(lane8 == 2, jnp.sum(chosen, axis=1, keepdims=True), 0)
    for k in range(2):
        corner = jnp.zeros((1, H), jnp.int32)
        for t in range(S):
            corner = corner + hit[t:t + 1] * offset[t, k:k + 1, :]
        out = jnp.where(lane8 == k, jnp.sum(chosen * corner, axis=1, keepdims=True), out)
    table[2 * N:2 * N + S] = out


def reorder(x, pick):
    def terms(v):
        hi, rest = split(v)
        rest = v - hi.astype(F32)
        mid, low = split(rest)
        return hi, mid, low

    p, pt = pick[0], pick[1]
    a, b, c = terms(x)
    y = mm(p, a) + (mm(p, b) + mm(p, c))
    a, b, c = terms(y)
    return mm(a, pt) + (mm(b, pt) + mm(c, pt))


def kernel(count, owner, offset, given, mask, measured, tab_in, pick, step, resid,
           f, pup, img, r1a, r1b, p2, r2, wla, wlb, sb, wret, keep, edge, halo, q0, q1, h2, meas, back, spectrum, tab, last, table, tabs, ax, arx, ary, amid,
           sem, sem4, asem, lsem):
    tx, ty = lax.axis_index("tx"), lax.axis_index("ty")
    z, y = tx // 4, tx % 4
    zd = [z] + [lax.rem(z + d, 4) for d in range(1, 4)]
    yd = [y] + [lax.rem(y + d, 4) for d in range(1, 4)]
    tile = [[zd[d] * 4 + y for d in range(4)], [z * 4 + yd[d] for d in range(4)]]
    across, along, atile = [zd, yd], [yd, zd], [tile[1], tile[0]]
    r1, wl = (r1a, r1b), (wla, wlb)
    tx_dev = [{"tx": lax.rem(tx + d, 16)} for d in range(16)]
    ty_dev = [{"ty": lax.rem(ty + d, 8)} for d in range(8)]
    edge_dev = [ty_dev[7], ty_dev[1], tx_dev[15], tx_dev[1]]

    def remote(src, dst, send, recv, dev):
        return pltpu.make_async_remote_copy(
            src_ref=src, dst_ref=dst, send_sem=send, recv_sem=recv, device_id=dev, device_id_type=MESH)

    def wait_sent(ref, s):
        remote(ref, ref, s, s, tx_dev[1]).wait_send()

    def wait_got(ref, s):
        remote(ref, ref, s, s, tx_dev[1]).wait_recv()

    def al(x, k):
        return pl.multiple_of(x * k, 8)

    def line_rows(half, d):
        return pl.ds(half * H + al(across[half][d], 32), 32)

    def sum_start(k):
        for d in range(1, 16):
            remote(ax.at[k], arx.at[k, d], asem.at[k, 0], asem.at[k, 1], tx_dev[d]).start()

    def sum_turn(k):
        wait_sent(arx.at[k, 1:16], asem.at[k, 0])
        wait_got(arx.at[k, 1:16], asem.at[k, 1])
        acc = ax[k]
        for d in range(1, 16):
            acc = acc + arx[k, d]
        amid[k] = acc
        for d in range(1, 8):
            remote(amid.at[k], ary.at[k, d], asem.at[k, 2], asem.at[k, 3], ty_dev[d]).start()

    def sum_end(k):
        wait_sent(ary.at[k, 1:8], asem.at[k, 2])
        wait_got(ary.at[k, 1:8], asem.at[k, 3])
        acc = amid[k]
        for d in range(1, 8):
            acc = acc + ary[k, d]
        return jnp.sum(acc, axis=1, keepdims=True)

    def halo_start(ph, v):
        pack_edges(v, edge.at[ph])
        for i, dst in enumerate((1, 0, 3, 2)):
            remote(edge.at[ph, i], halo.at[ph, dst], sem.at[ph, 0, 0], sem.at[ph, 0, 1], edge_dev[i]).start()

    def halo_end(ph):
        wait_sent(edge.at[ph], sem.at[ph, 0, 0])
        wait_got(halo.at[ph], sem.at[ph, 0, 1])
        for i, inside in enumerate((ty > 0, ty < 7, tx > 0, tx < 15)):
            halo[ph, i] = jnp.where(inside, halo[ph, i], 0.0)

    def send1(ph, q, low, count):
        if count == 1:
            src, dst = lambda rows: img.at[q, low, rows, :], lambda half, d: r1[q].at[ph, half, 4 - d, low]
        else:
            part = pl.ds(low, count)
            src, dst = lambda rows: img.at[q, part, rows, :], lambda half, d: r1[q].at[ph, half, 4 - d, part]
        for d in ORDER:
            for half in range(2):
                remote(src(line_rows(half, d)), dst(half, d), sem.at[ph, q, 2], sem.at[ph, q, 3],
                       {"tx": tile[half][d]}).start()

    def keep_own(ph, s):
        for q in range(2):
            for half in range(2):
                r1[q][ph, half, 0, s] = img[q, s, line_rows(half, 0), :]

    def send_meas():
        for q in range(2):
            for d in ORDER:
                for half in range(2):
                    remote(meas.at[q, line_rows(half, d), :], r1[q].at[0, half, 4 - d, S],
                           sem.at[0, q, 10], sem.at[0, q, 11], {"tx": tile[half][d]}).start()
            for half in range(2):
                r1[q][0, half, 0, S] = meas[q, line_rows(half, 0), :]

    def transforms(ph, low, high, image, turn=None):
        def body(s, _):
            image(s)
            send1(ph, 0, s, 1)

            @pl.when(s == CUT - 1)
            def _():
                send1(ph, 1, 0, CUT)

            keep_own(ph, s)
            if turn is not None:
                pl.when(s == 5)(turn)
            return 0

        lax.fori_loop(low, high, body, 0)
        if high == S:
            send1(ph, 1, CUT, S - CUT)

    def sums(ph, q):
        wait_sent(img.at[q, 0:6], sem.at[ph, q, 2])
        wait_got(r1[q].at[ph, :, 1:4, 0:S], sem.at[ph, q, 3])
        if ph == 0:
            wait_sent(r1[q].at[ph, :, 1:4, S], sem.at[ph, q, 10])
            wait_got(r1[q].at[ph, :, 1:4, S], sem.at[ph, q, 11])

        def partial(c, _):
            for half in range(2):
                acc = r1[q][ph, half, 0, slot_at(tile[half][0], c)]
                for d in range(1, 4):
                    acc = acc + r1[q][ph, half, d, slot_at(tile[half][d], c)]
                p2[q, half, :, c] = acc.reshape(4, 8, H)
            return 0

        lax.fori_loop(0, N, partial, 0, unroll=4)
        if ph == 0:
            for half in range(2):
                for d in range(4):
                    p2[q, half, :, tile[half][d]] -= r1[q][ph, half, d, S].reshape(4, 8, H)
        for d in ORDER:
            for half in range(2):
                remote(p2.at[q, half, along[half][d]], r2.at[ph, q, half, 4 - d],
                       sem.at[ph, q, 4], sem.at[ph, q, 5], {"tx": atile[half][d]}).start()

    def sums_end(ph, q, fix):
        wait_sent(r2.at[ph, q, :, 1:4], sem.at[ph, q, 4])
        wait_got(r2.at[ph, q, :, 1:4], sem.at[ph, q, 5])
        for half in range(2):
            w = (p2[q, half, along[half][0]] + r2[ph, q, half, 1]) + (r2[ph, q, half, 2] + r2[ph, q, half, 3])
            wl[q][ph, half, along[half][0]] = fix(q, half, w)
        for d in ORDER:
            for half in range(2):
                part = wl[q].at[ph, half, along[half][0]]
                remote(part, part, sem.at[ph, q, 6], sem.at[ph, q, 7], {"tx": atile[half][d]}).start()

    def got3(ph, q):
        wait_sent(wl[q].at[ph, :, 0:3], sem.at[ph, q, 6])
        wait_got(wl[q].at[ph, :, 0:3], sem.at[ph, q, 7])

    def stage4(ph, q, low, high):
        for s in range(low, high):
            for half in range(2):
                for d in range(4):
                    piece = wl[q][ph, half, :, cap_at(tile[half][d], s)].reshape(32, H)
                    if d == 0:
                        wret[ph, s, q, line_rows(half, 0), :] = piece
                    else:
                        sb[half, d - 1, s, q] = piece

    def send4(ph, q, g):
        low, high = GROUPS[g]
        for d in ORDER:
            for half in range(2):
                if q is None:
                    src, dst = sb.at[half, d - 1, low:high], wret.at[ph, low:high, :, line_rows(half, 0), :]
                else:
                    src, dst = sb.at[half, d - 1, low:high, q], wret.at[ph, low:high, q, line_rows(half, 0), :]
                remote(src, dst, sem.at[ph, 0, 8], sem4.at[ph, g], {"tx": tile[half][d]}).start()

    def give_back(ph):
        got3(ph, 0)
        stage4(ph, 0, *GROUPS[0])
        send4(ph, 0, 0)
        got3(ph, 1)
        stage4(ph, 1, *GROUPS[0])
        send4(ph, 1, 0)
        for g in range(1, len(GROUPS)):
            for q in range(2):
                stage4(ph, q, *GROUPS[g])
            send4(ph, None, g)

    def adjoint(ph, out, sign, late=()):
        back[1] = jnp.zeros((2, B, B), F32)

        def add_in(s, which):
            r, c = corner(s)
            deposit(out, s, r, c, pup, [[back[which, part, k * H:(k + 1) * H, :] for k in range(2)] for part in range(2)])

        def body(s, _):
            for g, (low, high) in enumerate(GROUPS):
                @pl.when(s == low)
                def _():
                    wait_got(wret.at[ph, low:high, :, 0:192, :], sem4.at[ph, g])

            for step_no, action in late:
                pl.when(s == step_no)(action)
            odd = lax.rem(s, 2)
            add_in(jnp.maximum(s - 1, 0), 1 - odd)
            w = [wret[ph, s, q] * (2.0 * sign) for q in range(2)]
            parts = backward(f, s, w, tab)
            for part in range(2):
                for k in range(2):
                    back[odd, part, k * H:(k + 1) * H, :] = parts[part][k]
            return 0

        lax.fori_loop(0, S, body, 0)
        add_in(S - 1, (S - 1) % 2)
        wait_sent(sb, sem.at[ph, 0, 8])

    def slot_at(a, c):
        return tabs[a, ty * N + c]

    def cap_at(a, s):
        return tabs[N + a, s]

    def corner(s):
        return tabs[2 * N + s, 0], tabs[2 * N + s, 1]

    bar = pltpu.get_barrier_semaphore()
    for dev in tx_dev[1:] + ty_dev[1:]:
        pl.semaphore_signal(bar, inc=1, device_id=dev, device_id_type=MESH)
    loads = [pltpu.make_async_copy(given, spectrum, lsem.at[1]), pltpu.make_async_copy(tab_in, tab, lsem.at[2])]
    for copy in loads:
        copy.start()
    for ph in range(3):
        for half in range(2):
            for d in range(4):
                for q in range(2):
                    r1[q][ph, half, d, S + 1] = jnp.zeros((32, H), F32)
    route(ty, tx, count, owner, offset, table)
    to_scalar = pltpu.make_async_copy(table, tabs, lsem.at[0])
    to_scalar.start()
    ordered = reorder(measured[0], pick)
    for q in range(2):
        meas[q] = ordered[:, q * H:(q + 1) * H]
    ax[...] = jnp.zeros((2, 8, H), F32)
    for copy in [to_scalar] + loads:
        copy.wait()

    def fields(s):
        r, c = corner(s)
        base = mask[...].astype(F32)
        rolled = pltpu.roll(pltpu.roll(base, jnp.bitwise_and(r, B - 1), axis=0), jnp.bitwise_and(c, B - 1), axis=1)
        pup[s] = rolled * tabs[2 * N + s, 2].astype(F32)
        g = forward(spectrum, s, r, c, pup, tab)
        for q in range(2):
            f[s, q] = g[q]
            img[q, s] = g[q][:, :H] * g[q][:, :H] + g[q][:, H:] * g[q][:, H:]

    def image_of(v):
        def image(s):
            r, c = corner(s)
            g = forward(v, s, r, c, pup, tab)
            for q in range(2):
                fq = f[s, q]
                img[q, s] = 2.0 * (fq[:, :H] * g[q][:, :H] + fq[:, H:] * g[q][:, H:])

        return image

    fields(0)
    pl.semaphore_wait(bar, 22)
    send_meas()
    send1(0, 0, 0, 1)
    keep_own(0, 0)
    transforms(0, 1, S, fields)
    halo_start(0, spectrum)
    sums(0, 0)
    sums(0, 1)
    halo_end(0)
    laplace_to(q0, spectrum, halo.at[0], -REG)
    for q in range(2):
        sums_end(0, q, lambda q, half, w: w)
    give_back(0)
    adjoint(0, q0, -1.0)

    transforms(1, 0, S, image_of(q0))
    halo_start(1, q0)
    sums(1, 0)
    sums(1, 1)
    halo_end(1)
    laplace_to(q1, q0, halo.at[1], REG)

    def keep_first(q, half, w):
        keep[q, half] = w
        k = 2 + 2 * q + half
        ax[0, k:k + 1, :] = lanes((w * w).reshape(N * 8, H))
        return w

    for q in range(2):
        sums_end(1, q, keep_first)
    ax[0, 0:1, :] = dot_rows(whole(q0), whole(q0))
    ax[0, 1:2, :] = dot_rows(whole(q0), whole(q1))
    give_back(1)
    adjoint(1, q1, 1.0)

    transforms(2, 0, 2, image_of(q1))
    ax[0, 6:7, :] = dot_rows(whole(q1), whole(q1))
    sum_start(0)
    transforms(2, 2, S, image_of(q1), lambda: sum_turn(0))
    halo_start(2, q1)
    sums(2, 0)
    sums(2, 1)
    red = sum_end(0)

    def heading_image(red):
        return (red[1:2] + red[2:3]) + ((red[3:4] + red[4:5]) + red[5:6])

    res, hah, aa = red[0:1], heading_image(red), red[6:7]
    alpha = res / hah
    beta = (res - 2.0 * alpha * hah + alpha * alpha * aa) / res
    alpha_s, one_s = alpha[0, 0], (1.0 + beta)[0, 0]
    halo_end(2)
    for i in range(4):
        halo[2, i] = one_s * halo[1, i] - alpha_s * halo[2, i]
    for part in range(2):
        h2[part] = one_s * q0[part] - alpha_s * q1[part]
        q1[part] = q0[part] - alpha_s * q1[part]
    laplace_to(resid, h2, halo.at[2], REG)

    def second(q, half, w):
        w = one_s * keep[q, half] - alpha_s * w
        k = 2 + 2 * q + half
        ax[1, k:k + 1, :] = lanes((w * w).reshape(N * 8, H))
        return w

    for q in range(2):
        sums_end(2, q, second)
    ax[1, 0:1, :] = dot_rows(whole(q1), whole(q1))
    ax[1, 1:2, :] = dot_rows(whole(h2), whole(resid))
    sum_start(1)
    give_back(2)

    def close_step():
        red = sum_end(1)
        ratio = red[0:1] / heading_image(red)
        last[...] = jnp.broadcast_to(ratio, (1, H))
        a = ratio[0, 0]
        for part in range(2):
            step[part] = alpha_s * q0[part] + a * h2[part]

    adjoint(2, resid, 1.0, ((2, lambda: sum_turn(1)), (6, close_step)))
    a = last[0:1, 0:1][0, 0]
    for part in range(2):
        resid[part] = q1[part] - a * resid[part]


def on_device(spectrum, measured, pupil_mask, led_count, led_owner, led_offset):
    pick = np.zeros((B, B), np.float32)
    for p in range(2):
        pick[p * H + np.arange(H), 2 * np.arange(H) + p] = 1.0
    pick = jnp.asarray(np.stack([pick, pick.T]).astype(jnp.bfloat16))
    dma = pltpu.SemaphoreType.DMA
    out = pltpu.VMEM((2, T, T), F32)

    def vm(*shape):
        return pltpu.VMEM(shape, F32)

    return pl.pallas_call(
        kernel, out_shape=(out, out), in_specs=[VM, VM, VM, ANY, VM, VM, ANY, VM], out_specs=(VM, VM),
        scratch_shapes=[
            vm(S, 2, B, B), vm(S, B, B), vm(2, S, B, H), vm(3, 2, 4, S + 2, 32, H), vm(3, 2, 4, S + 2, 32, H), vm(2, 2, 4, N, 8, H),
            vm(3, 2, 2, 4, N, 8, H), vm(3, 2, 4, N, 8, H), vm(3, 2, 4, N, 8, H), vm(2, 3, S, 2, 32, H), vm(3, S, 2, B, H),
            vm(2, 2, N, 8, H), vm(3, 4, 2, T), vm(3, 4, 2, T), vm(2, T, T), vm(2, T, T), vm(2, T, T), vm(2, B, H), vm(2, 2, B, B), vm(2, T, T), pltpu.VMEM((2, 4, B, B), BF), vm(1, H),
            pltpu.VMEM((40, H), jnp.int32), pltpu.SMEM((40, H), jnp.int32),
            vm(2, 8, H), vm(2, 16, 8, H), vm(2, 8, 8, H), vm(2, 8, H),
            dma((3, 2, 12)), dma((3, len(GROUPS))), dma((2, 4)), dma((3,)),
        ],
        compiler_params=pltpu.CompilerParams(collective_id=0, has_side_effects=True, vmem_limit_bytes=LIMIT),
        name="update",
    )(led_count.reshape(1, -1), led_owner.T, led_offset.transpose(1, 2, 0), spectrum, pupil_mask, measured,
      tables(), pick)


def solution(mesh):
    placed = (P(None, "ty", "tx"), P(("ty", "tx"), None, None), P(), P(), P(), P())
    return jax.shard_map(
        on_device, mesh=mesh, in_specs=placed,
        out_specs=(P(None, "ty", "tx"), P(None, "ty", "tx")), check_vma=False)
```
